512 devices in a mesh: kv: 8 (over x, core), pg: 64 (over y, z).
Axes of the slice: x: 4, y: 4, z: 16, core: 2. Of those that a mesh axis runs over, the one named last changes fastest.
Arguments:
- residual_in: bfloat16 [4096, 1536], P('pg', 'kv'), as said below
- queries: bfloat16 [256, 1536], P('pg', 'kv'), as said below
- prefill_attn: bfloat16 [3840, 1536], P('pg', 'kv'), may hold values from -1.1953125 to 1.1953125
- kv_cache: bfloat16 [1024, 8, 128, 128], P('pg', 'kv'), as said below
- page_table: int32 [256, 4], replicated, may hold values from 0 to 1023, as said below
- lengths: int32 [256], replicated, may hold values from 2 to 512, as said below
- out_weight: bfloat16 [1536, 1536], P('kv'), may hold values from -0.75 to 0.75
- norm_gain_in: float32 [1536], P('kv'), may hold values from 0.25 to 1.75
- norm_gain_out: float32 [1536], P('kv'), may hold values from 0.25 to 1.75
- expert_ids: int32 [4096, 8], P('pg'), may hold values from 0 to 39, all different within a row; in each aligned block of 64 rows (0 to 63, 64 to 127, ...) at most 16 rows name the same one
- route_weight: float32 [4096, 8], P('pg'), may hold values from 0.05 to 1
- slot_table: int32 [40, 2], replicated, may hold values from 0 to 63, as said below
- w_gate_up: bfloat16 [64, 1536, 1024], P('pg', 'kv'), as said below
- w_down: bfloat16 [64, 512, 1536], P('pg', None, 'kv'), as said below
Outputs:
- layer_out: bfloat16 [4096, 1536], P('pg', 'kv')
The draws below stay inside these ranges and needn't reach their ends.
Inputs may be any that keep to these rules, and one draw needn't show every extreme that they name: `page_table`: every page of 0 to 1023 appears exactly once in the table. `lengths`: some request has exactly 512 cached tokens. `slot_table`: row e lists the slots of expert e; each slot of 0 to 63 belongs to exactly one expert; an expert with a single slot repeats it. `w_gate_up`: slots of the same expert carry equal weights; entries lie within -0.2 and 0.2. `w_down`: slots of the same expert carry equal weights; entries lie within -0.3 and 0.3. `queries`: entries lie within -60 and 60. `kv_cache`: entries lie within -6 and 6. `residual_in`: entries lie within -50 and 50. `expert_ids`: in each aligned block of 64 rows no expert is named more than 16 times.
All inputs are finite; a program needn't handle non-finite values.
Results may differ from the reference program's by a relative error of at most 0.02.
Values may be sent and summed in bfloat16 or wider, within the bound.
A program may use at most 128 MiB of HBM per device.

```python
import math
import jax
import jax.numpy as jnp
import numpy as np
from jax import lax

D = 1536
QUERY_HEADS = 24
KEY_VALUE_HEADS = 8
HEAD_SIZE = 64
EXPERT_COUNT = 40
FF = 512
TOPK = 8
PAGE_TOKENS = 128
MAXP = 4
RMAX = 2
REQ_DEV = 4
PRE_DEV = 60
ROWS_DEV = 64
DECODE_REQUESTS = 256
PRE = 3840
TOKENS = 4096
CACHE_PAGES = 1024
EXPERT_SLOTS = 64
CAP = 16
N_KV = 8
N_PG = 64


def page_layout(key):
    sort_order = jax.random.permutation(jax.random.fold_in(key, 11), CACHE_PAGES)
    return sort_order.reshape(DECODE_REQUESTS, MAXP).astype(jnp.int32)


def draw_page_table(key, part):
    return page_layout(key)


def draw_lengths(key, part):
    base = jax.random.randint(jax.random.fold_in(key, 12), (DECODE_REQUESTS,), 2, MAXP * PAGE_TOKENS + 1)
    longest = jax.random.randint(jax.random.fold_in(key, 13), (), 0, DECODE_REQUESTS)
    return base.at[longest].set(MAXP * PAGE_TOKENS).astype(jnp.int32)


def cache_values(key):
    array_shape = (CACHE_PAGES, KEY_VALUE_HEADS, PAGE_TOKENS, 2 * HEAD_SIZE)
    cache = jnp.clip(jax.random.normal(jax.random.fold_in(key, 21), array_shape, jnp.float32), -6.0, 6.0)
    return cache


def draw_kv_cache(key, part):
    return cache_values(key).astype(jnp.bfloat16)


def draw_queries(key, part):
    array_shape = (DECODE_REQUESTS, QUERY_HEADS * HEAD_SIZE)
    return (2.0 * jnp.clip(jax.random.normal(jax.random.fold_in(key, 22), array_shape, jnp.float32), -6.0, 6.0)).astype(jnp.bfloat16)


def draw_residual_in(key, part):
    row_scale = jnp.exp(jax.random.uniform(jax.random.fold_in(key, 41), (TOKENS, 1), jnp.float32, math.log(0.3), math.log(3.0)))
    column = jnp.arange(D, dtype=jnp.float32)[None, :] / D
    col_scale = 0.3 * jnp.exp(column * math.log(10.0)) * jnp.exp(jax.random.uniform(jax.random.fold_in(key, 42), (1, D), jnp.float32, -0.3, 0.3))
    noise = jnp.clip(jax.random.normal(jax.random.fold_in(key, 43), (TOKENS, D), jnp.float32), -4.0, 4.0)
    return (noise * row_scale * col_scale).astype(jnp.bfloat16)


def slot_layout(key):
    sort_order = jax.random.permutation(jax.random.fold_in(key, 31), EXPERT_SLOTS).astype(jnp.int32)
    additional = jax.random.permutation(jax.random.fold_in(key, 32), EXPERT_COUNT).astype(jnp.int32)
    slot_holders = jnp.concatenate([jnp.arange(EXPERT_COUNT, dtype=jnp.int32), additional[:EXPERT_SLOTS - EXPERT_COUNT]])
    expert_of_slot = jnp.zeros((EXPERT_SLOTS,), jnp.int32).at[sort_order].set(slot_holders)
    return (sort_order, additional, expert_of_slot)


def draw_slot_table(key, part):
    sort_order, additional, expert_of_slot = slot_layout(key)
    placement_index = jnp.argsort(additional, stable=True).astype(jnp.int32)
    primary_slot = sort_order[:EXPERT_COUNT]
    spare_slot = sort_order[jnp.clip(EXPERT_COUNT + placement_index, 0, EXPERT_SLOTS - 1)]
    secondary_slot = jnp.where(placement_index < EXPERT_SLOTS - EXPERT_COUNT, spare_slot, primary_slot)
    return jnp.stack([primary_slot, secondary_slot], axis=1).astype(jnp.int32)


def draw_w_gate_up(key, part):
    sort_order, additional, expert_of_slot = slot_layout(key)
    base = jnp.clip(jax.random.normal(jax.random.fold_in(key, 33), (EXPERT_COUNT, D, 2 * FF), jnp.float32), -5.0, 5.0)
    return (base * D ** (-0.5))[expert_of_slot].astype(jnp.bfloat16)


def draw_w_down(key, part):
    sort_order, additional, expert_of_slot = slot_layout(key)
    base = jnp.clip(jax.random.normal(jax.random.fold_in(key, 34), (EXPERT_COUNT, FF, D), jnp.float32), -5.0, 5.0)
    return (base * FF ** (-0.5))[expert_of_slot].astype(jnp.bfloat16)


def block_scale(stream_key, shape, split, least, largest):
    def one(dim, parts):
        heights = jax.random.uniform(jax.random.fold_in(jax.random.fold_in(stream_key, 6), dim), (parts,), jnp.float32, least / len(split), largest / len(split))
        return jnp.repeat(jnp.exp(heights), shape[dim] // parts).reshape((-1,) + (1,) * (len(shape) - dim - 1))

    level = one(*split[0])
    for cut in split[1:]:
        level = level * one(*cut)
    return level


def deal_out(key, own, number, rows, number_of, top, limit, slope):
    sequence = jax.random.permutation(key, number_of)
    crowded, usual = load_shares(number_of, rows * top, limit, slope, True), load_shares(number_of, rows * top, limit, slope, False)
    places = jnp.arange(number_of)

    def named(sizes, rotation):
        used = int((sizes > 0).sum())
        fixed = max(1, used // 4)
        shifted = fixed + (places - fixed + rotation * (used - fixed)) % max(1, number_of - fixed)
        return jnp.zeros((number_of,), jnp.int32).at[sequence[jnp.where(places < fixed, places, shifted)]].set(jnp.asarray(sizes, jnp.int32))

    sizes = jnp.where(number % 4 == 0, named(crowded, number // 4), named(usual, number - number // 4 - 1))
    mixed = jax.random.permutation(jax.random.fold_in(own, 3), number_of)
    source_of, taker = mixed[0:number_of // 2 * 2:2], mixed[1:number_of // 2 * 2:2]
    room = jnp.minimum(sizes[source_of] - 1, limit - sizes[taker]) // 2
    room = jnp.where((source_of == sequence[0]) | (taker == sequence[0]) | (sizes[taker] == 0), 0, jnp.maximum(room, 0))
    shifted = jax.random.randint(jax.random.fold_in(own, 4), (number_of // 2,), 0, 1 << 20) % (room + 1)
    sizes = sizes.at[source_of].add(-shifted).at[taker].add(shifted)
    labels = jnp.searchsorted(jnp.cumsum(sizes), jnp.arange(rows * top), side="right").astype(jnp.int32)
    listing = labels.reshape(top, rows).T
    listing = listing[jax.random.permutation(jax.random.fold_in(own, 1), rows)]
    rotation = jax.random.randint(jax.random.fold_in(own, 2), (rows, 1), 0, top)
    return jnp.take_along_axis(listing, (jnp.arange(top)[None, :] + rotation) % top, axis=1)


def load_shares(count, total, limit, slope, full):
    loads = [(1 << 20) // math.isqrt(standing ** slope) + 1 for standing in range(1, count + 1)]
    largest = limit if full else min(limit, max(-(-total // count), total * loads[0] // sum(loads)))
    least = 1 if total - largest >= count - 1 else 0
    holding, surplus = [largest] + [least] * (count - 1), total - largest - least * (count - 1)
    while surplus > 0:
        free = [i for i in range(1, count) if holding[i] < largest] or [i for i in range(1, count) if holding[i] < limit]
        mass, remaining = sum([loads[i] for i in free]), surplus
        for i in free:
            extra = min(limit - holding[i], max(1, remaining * loads[i] // mass), surplus)
            holding[i] = holding[i] + extra
            surplus = surplus - extra
    return np.array(holding)


def gaussian(key, extent, scale, most, split=(), kind=jnp.bfloat16):
    level = block_scale(key, extent, split, -0.22, 0.18) if split else 1.0
    values = jax.random.normal(key, extent, jnp.float32) * scale * level
    return jnp.minimum(jnp.maximum(values, -most), most).astype(kind)


def setup_inputs(seed: int = 0) -> dict:
    key_of = jax.random.split(jax.random.key(seed), 15)
    residual_in = draw_residual_in(jax.random.fold_in(key_of[14], 71), 0)
    queries = draw_queries(jax.random.fold_in(key_of[14], 71), 0)
    prefill_attn = gaussian(key_of[2], (PRE, QUERY_HEADS * HEAD_SIZE), 0.2, 1.1953125, ((0, 64), (1, 8)))
    kv_cache = draw_kv_cache(jax.random.fold_in(key_of[14], 71), 0)
    page_table = draw_page_table(jax.random.fold_in(key_of[14], 71), 0)
    lengths = draw_lengths(jax.random.fold_in(key_of[14], 71), 0)
    out_weight = gaussian(key_of[6], (QUERY_HEADS * HEAD_SIZE, D), HEAD_SIZE ** -0.5, 0.75, ((0, 8),))
    norm_gain_in = jnp.clip(1.0 + 0.15 * jax.random.normal(key_of[7], (D,), jnp.float32), 0.25, 1.75)
    norm_gain_out = jnp.clip(1.0 + 0.15 * jax.random.normal(key_of[8], (D,), jnp.float32), 0.25, 1.75)
    expert_ids_keys = jax.random.split(jax.random.fold_in(key_of[9], 1), TOKENS // ROWS_DEV)
    expert_ids_turns = jax.random.permutation(jax.random.fold_in(key_of[9], 3), TOKENS // ROWS_DEV)
    expert_ids = jax.vmap(lambda own, number: deal_out(jax.random.fold_in(key_of[9], 2), own, number, ROWS_DEV, EXPERT_COUNT, TOPK, CAP, 2))(expert_ids_keys, expert_ids_turns).reshape((TOKENS, TOPK))
    route_weight = jnp.clip(jnp.exp(math.log(1.0) - 2.9957323 * jax.random.uniform(key_of[10], (TOKENS, TOPK), jnp.float32) ** block_scale(key_of[10], (TOKENS, TOPK), ((0, 64),), -0.2, 0.2)), 0.05, 1.0)
    slot_table = draw_slot_table(jax.random.fold_in(key_of[14], 71), 0)
    w_gate_up = draw_w_gate_up(jax.random.fold_in(key_of[14], 71), 0)
    w_down = draw_w_down(jax.random.fold_in(key_of[14], 71), 0)
    return {"residual_in": residual_in, "queries": queries, "prefill_attn": prefill_attn, "kv_cache": kv_cache, "page_table": page_table, "lengths": lengths, "out_weight": out_weight, "norm_gain_in": norm_gain_in, "norm_gain_out": norm_gain_out, "expert_ids": expert_ids, "route_weight": route_weight, "slot_table": slot_table, "w_gate_up": w_gate_up, "w_down": w_down}


NEG_FILL = -1e+30
EPSILON = 1e-06

def decode_attention(queries, kv_cache, page_table, lengths):
    head_group = QUERY_HEADS // KEY_VALUE_HEADS

    def one_request(lookup_index):
        pages = page_table[lookup_index]
        block = kv_cache[pages].astype(jnp.float32)
        keys = block[..., :HEAD_SIZE]
        values = block[..., HEAD_SIZE:]
        query_vector = queries[lookup_index].astype(jnp.float32).reshape(KEY_VALUE_HEADS, head_group, HEAD_SIZE)
        scores = jnp.einsum('kgd,pktd->pkgt', query_vector, keys) * HEAD_SIZE ** (-0.5)
        positions = jnp.arange(MAXP, dtype=jnp.int32)[:, None] * PAGE_TOKENS + jnp.arange(PAGE_TOKENS, dtype=jnp.int32)[None, :]
        live = (positions < lengths[lookup_index])[:, None, None, :]
        masked = jnp.where(live, scores, NEG_FILL)
        page_max = lax.optimization_barrier(jnp.max(masked, axis=3))
        probs = jnp.where(live, jnp.exp(masked - page_max[..., None]), 0.0)
        probs = lax.optimization_barrier(probs.astype(jnp.bfloat16)).astype(jnp.float32)
        page_sum = lax.optimization_barrier(jnp.sum(probs, axis=3))
        page_acc = jnp.einsum('pkgt,pktd->pkgd', probs, values)
        highest = lax.optimization_barrier(jnp.max(page_max, axis=0))
        weight = jnp.exp(page_max - highest[None])
        total = lax.optimization_barrier(jnp.sum(weight * page_sum, axis=0))
        result = lax.optimization_barrier(jnp.sum(weight[..., None] * page_acc, axis=0)) / total[..., None]
        return result.reshape(-1)
    return lax.map(one_request, jnp.arange(DECODE_REQUESTS, dtype=jnp.int32)).astype(jnp.bfloat16)

def blockwise(left, right, blocks):
    width = left.shape[1] // blocks
    summed = jnp.zeros((left.shape[0], right.shape[1]), jnp.float32)
    for block_index in range(blocks):
        part = jnp.dot(left[:, block_index * width:(block_index + 1) * width], right[block_index * width:(block_index + 1) * width], preferred_element_type=jnp.float32)
        part = lax.optimization_barrier(part.astype(jnp.bfloat16)).astype(jnp.float32)
        summed = summed + part
    return summed

def rms_norm(values, gain):
    return values * lax.rsqrt(lax.optimization_barrier(jnp.mean(values * values, axis=1, keepdims=True)) + EPSILON) * gain

def reference(residual_in, queries, prefill_attn, kv_cache, page_table, lengths, out_weight, norm_gain_in, norm_gain_out, expert_ids, route_weight, slot_table, w_gate_up, w_down):
    attn_dec = decode_attention(queries, kv_cache, page_table, lengths)
    attn_rows = jnp.concatenate([attn_dec.reshape(N_PG, REQ_DEV, QUERY_HEADS * HEAD_SIZE), prefill_attn.reshape(N_PG, PRE_DEV, QUERY_HEADS * HEAD_SIZE)], axis=1).reshape(TOKENS, QUERY_HEADS * HEAD_SIZE)
    middle = residual_in.astype(jnp.float32) + blockwise(attn_rows, out_weight, N_KV)
    normed = rms_norm(middle, norm_gain_in).astype(jnp.bfloat16)
    row_plus = jnp.arange(TOKENS, dtype=jnp.int32)[:, None] + jnp.arange(TOPK, dtype=jnp.int32)[None, :]
    target_slot = slot_table[expert_ids, row_plus % RMAX].reshape(-1).astype(jnp.int32)
    slot_rows = N_PG * CAP
    entry_list = TOKENS * TOPK
    match_count = (target_slot[:, None] == jnp.arange(EXPERT_SLOTS, dtype=jnp.int32)[None, :]).astype(jnp.int32)
    rank = lax.optimization_barrier(jnp.sum((jnp.cumsum(match_count, axis=0) - match_count) * match_count, axis=1)).astype(jnp.int32)
    token_position = (target_slot * slot_rows + rank).astype(jnp.int32)
    entry_lookup = jnp.full((EXPERT_SLOTS * slot_rows,), entry_list, jnp.int32).at[token_position].set(jnp.arange(entry_list, dtype=jnp.int32)).reshape(EXPERT_SLOTS, slot_rows)
    normed_pad = jnp.concatenate([normed, jnp.zeros((1, D), jnp.bfloat16)], axis=0)
    weight_pad = jnp.concatenate([route_weight.reshape(-1), jnp.zeros((1,), jnp.float32)], axis=0)

    def expert(carry, operands):
        entry_ids, gate_up_w, down_w = operands
        token_ids = (entry_ids // TOPK).astype(jnp.int32)
        picked = normed_pad[token_ids]
        gate_up = jnp.dot(picked, gate_up_w, preferred_element_type=jnp.float32)
        hidden = (jax.nn.silu(gate_up[:, :FF]) * gate_up[:, FF:]).astype(jnp.bfloat16)
        produced = jnp.dot(hidden, down_w, preferred_element_type=jnp.float32).astype(jnp.bfloat16)
        produced = lax.optimization_barrier(produced).astype(jnp.float32)
        carry = carry.at[token_ids].add(produced * weight_pad[entry_ids][:, None])
        return (carry, None)
    start = jnp.zeros((TOKENS + 1, D), jnp.float32)
    routed, unused = lax.scan(expert, start, (entry_lookup, w_gate_up, w_down))
    mixed = middle + routed[:TOKENS]
    return rms_norm(mixed, norm_gain_out).astype(jnp.bfloat16)
```

```python
import functools
import jax
import jax.numpy as jnp
from jax import lax
from jax.experimental import pallas as pl
from jax.experimental.pallas import tpu as pltpu
from jax.sharding import PartitionSpec as P

NEG_FILL = -1e30
EPSILON = 1e-06
OFFSET = 4096.0
MESH = pl.DeviceIdType.MESH
NY = 4
F32 = jnp.float32
BF16 = jnp.bfloat16


def iota(shape, dim):
    return lax.broadcasted_iota(jnp.int32, shape, dim)


def remote(src, dst, ssem, rsem, dev):
    return pltpu.make_async_remote_copy(
        src_ref=src,
        dst_ref=dst,
        send_sem=ssem,
        recv_sem=rsem,
        device_id=dev,
        device_id_type=MESH,
    )


def greet(ny, nz, nkv, yy, zz, kk):
    barrier = pltpu.get_barrier_semaphore()

    def z_body(d, c):
        peer = yy * nz + lax.rem(zz + d, nz)
        pl.semaphore_signal(barrier, inc=1, device_id={"pg": peer}, device_id_type=MESH)
        return c

    lax.fori_loop(1, nz, z_body, 0)
    for d in range(1, ny):
        peer = lax.rem(yy + d, ny) * nz + zz
        pl.semaphore_signal(barrier, inc=1, device_id={"pg": peer}, device_id_type=MESH)
    for d in range(1, nkv):
        peer = lax.rem(kk + d, nkv)
        pl.semaphore_signal(barrier, inc=1, device_id={"kv": peer}, device_id_type=MESH)
    pl.semaphore_wait(barrier, nz - 1 + ny - 1 + nkv - 1)


def to_tiles(rows, data):
    out = []
    for j in range(len(data) // 2):
        even, odd = data[2 * j], data[2 * j + 1]
        out.append(even[:, :128])
        out.append(even[:, 128:] + odd[:, :128])
        out.append(odd[:, 128:])
    return jnp.concatenate(out, axis=1)


def placement(parity, transposed=False):
    shape = (256, 192) if transposed else (192, 256)
    narrow, wide = (1, 0) if transposed else (0, 1)
    return (iota(shape, wide) == iota(shape, narrow) + 64 * parity).astype(BF16)


def stat_tile(x2):
    n = x2.shape[0]
    lane = iota((128, 256), 0) - 64
    head = iota((128, 256), 1) // 64
    pick = ((lane >= 0) & (lane < 9) & (lane % 3 == head) & (head < 3)).astype(BF16)
    spread = jnp.dot(x2, pick, preferred_element_type=F32)
    low = pltpu.roll(spread[:, :128], n - 4, 0)
    return jnp.where(iota((n, 128), 0) % 8 < 4, low, spread[:, 128:])


def split3(x):
    hi = x.astype(BF16).astype(F32)
    mid = (x - hi).astype(BF16).astype(F32)
    return hi, mid, x - hi - mid


def encode(acc, lse):
    n = acc.shape[0]
    sub, lane = iota((n, 128), 0) % 8, iota((n, 128), 1)
    down = pltpu.roll(lse, 4, 0)
    first = pltpu.roll(down, 64, 1)
    third = pltpu.roll(lse, 64, 1)
    which = (lane - 64) % 3
    value = jnp.where(which == 0, first, jnp.where(which == 1, down, third))
    hi, mid, lo = split3(value)
    part = (lane - 64) // 3
    stat = jnp.where(part == 0, hi, jnp.where(part == 1, mid, lo))
    is_stat = (sub >= 4) & (lane >= 64)
    return jnp.where(is_stat, jnp.where(lane < 73, stat, 0.0), acc).astype(BF16)


def merge(x):
    n, m, _ = x.shape
    flat = x.reshape(n * m, 128)
    lse = stat_tile(flat).reshape(n, m, 128)
    acc = flat.astype(F32).reshape(n, m, 128)
    top = jnp.max(lse, axis=0)
    weight = jnp.exp(lse - top[None])
    total = jnp.sum(weight, axis=0)
    return jnp.sum(weight * acc, axis=0) / total, top + jnp.log(total)


def attention_kernel(
    nz,
    nkv,
    q_ref,
    kv_ref,
    pt_ref,
    le_ref,
    pre_ref,
    w_ref,
    res_ref,
    gi_ref,
    go_ref,
    ids_ref,
    rw_ref,
    st_ref,
    wgu_ref,
    wd_ref,
    blk_ref,
    mid_ref,
    gout_ref,
    wgu_all,
    wd_all,
    qtile,
    qall,
    part,
    ybuf,
    zsend,
    zbuf,
    pre_s,
    proj,
    rsbuf,
    ressend,
    resbuf,
    gsend,
    gbuf,
    wds,
    s_q,
    r_q,
    s_qy,
    r_qy,
    s_py,
    r_py,
    s_pz,
    r_pz,
    s_rs,
    r_rs,
    s_res,
    r_res,
    s_g,
    r_g,
    s_wg,
    r_wg,
    s_wd,
    r_wd,
    l_w,
):
    ny = NY
    nx = nkv // 2
    pg, kk = lax.axis_index("pg"), lax.axis_index("kv")
    yy, zz = pg // nz, lax.rem(pg, nz)
    xx, cc = kk // 2, lax.rem(kk, 2)
    pages = kv_ref.shape[0]
    rows = pages * 8
    width = w_ref.shape[1]
    tops = ids_ref.shape[1]
    own_req = q_ref.shape[0]

    greet(ny, nz, nkv, yy, zz, kk)

    def z_peer(d):
        return lax.rem(zz + d, nz)

    def y_peer(d):
        return lax.rem(yy + d, ny)

    def k_peer(d):
        return lax.rem(kk + d, nkv)

    q32 = q_ref[...].astype(F32)
    qtile[...] = jnp.zeros_like(qtile)
    qtile[0:own_req, :] = q32[:, :128]
    qtile[4 : 4 + own_req, 0:64] = q32[:, 128:]
    qall[yy, zz] = qtile[...].astype(BF16)

    def q_copy(src_z, dst_z):
        return remote(
            qall.at[yy, src_z],
            qall.at[yy, src_z],
            s_q.at[dst_z],
            r_q.at[src_z],
            {"pg": yy * nz + dst_z},
        )

    def q_start(d, c):
        q_copy(zz, z_peer(d)).start()
        return c

    lax.fori_loop(1, nz, q_start, 0)

    def wg_copy(src_x, dst_x):
        return remote(
            wgu_ref.at[0],
            wgu_all.at[src_x],
            s_wg.at[dst_x],
            r_wg.at[src_x],
            {"kv": dst_x * 2 + cc},
        )

    def wd_copy(src_x, dst_x):
        return remote(
            wds, wd_all.at[src_x], s_wd.at[dst_x], r_wd.at[src_x], {"kv": dst_x * 2 + cc}
        )

    for d in range(1, nx):
        wg_copy(xx, lax.rem(xx + d, nx)).start()
    own_wg = pltpu.make_async_copy(wgu_ref.at[0], wgu_all.at[xx], l_w.at[0])
    own_wg.start()
    spread = placement(cc)
    wds[...] = jnp.dot(wd_ref[0], spread, preferred_element_type=F32).astype(BF16)
    for d in range(1, nx):
        wd_copy(xx, lax.rem(xx + d, nx)).start()
    own_wd = pltpu.make_async_copy(wds, wd_all.at[xx], l_w.at[1])
    own_wd.start()

    ressend[...] = (
        jnp.dot(res_ref[...], spread, preferred_element_type=F32)
        .astype(BF16)
        .reshape(ressend.shape)
    )
    gsend[...] = jnp.zeros_like(gsend)
    gsend[0:1, 0:192] = gi_ref[...]
    gsend[1:2, 0:192] = go_ref[...]
    gains = gsend[...]
    gsend[...] = jnp.where(cc == 1, pltpu.roll(gains, 64, 1), gains)

    def res_copy(src_k, dst_k):
        return remote(
            ressend.at[dst_k], resbuf.at[src_k], s_res.at[dst_k], r_res.at[src_k], {"kv": dst_k}
        )

    def g_copy(src_k, dst_k):
        return remote(gsend, gbuf.at[src_k], s_g.at[dst_k], r_g.at[src_k], {"kv": dst_k})

    for d in range(1, nkv):
        res_copy(kk, k_peer(d)).start()
        g_copy(kk, k_peer(d)).start()
    resbuf[kk] = ressend[kk]
    gbuf[kk] = gsend[...]

    pre_s[0:own_req, :] = jnp.zeros((own_req, pre_s.shape[1]), F32)
    pre_s[own_req:, :] = pre_ref[...].astype(F32)
    done = jnp.dot(pre_s[...].astype(BF16), w_ref[...], preferred_element_type=F32)
    proj[...] = done.astype(BF16).reshape(proj.shape)
    head_rows = done[0:8]

    def rs_copy(src_k, dst_k):
        return remote(
            proj.at[dst_k], rsbuf.at[src_k], s_rs.at[dst_k], r_rs.at[src_k], {"kv": dst_k}
        )

    for k in range(1, nkv):

        @pl.when(kk != k)
        def _():
            rs_copy(kk, k).start()

    page_row = iota((rows, 1), 0) // 8
    head = iota((rows, 1), 0) % 8
    mine = pt_ref[...] == page_row + pg * pages
    place = iota(mine.shape, 1).astype(F32)
    entry = jnp.sum(jnp.where(mine, place, 0.0), axis=1, keepdims=True)
    cached = jnp.sum(jnp.where(mine, le_ref[...], 0.0), axis=1, keepdims=True)
    owner = jnp.floor(entry * 0.25)
    limit = cached - (entry - 4.0 * owner) * 128.0
    owner_pg = jnp.floor(owner * 0.25)
    owner_col = 8.0 * owner_pg + (owner - 4.0 * owner_pg)
    wanted = owner_col + jnp.where(head == 2, 4.0, 0.0)
    npg = ny * nz
    select = (iota((rows, npg * 8), 1).astype(F32) == wanted) & (head < 3)
    select = select.astype(BF16)

    def q_wait(d, c):
        q_copy(z_peer(d), zz).wait_recv()
        return c

    lax.fori_loop(1, nz, q_wait, 0)

    def qy_copy(src_y, dst_y):
        return remote(
            qall.at[src_y], qall.at[src_y], s_qy.at[dst_y], r_qy.at[src_y], {"pg": dst_y * nz + zz}
        )

    for d in range(1, ny):
        qy_copy(yy, y_peer(d)).start()
    for d in range(1, ny):
        qy_copy(y_peer(d), yy).wait_recv()

    lane = iota((rows, 128), 1)
    queries = jnp.dot(select, qall[...].reshape(npg * 8, 128), preferred_element_type=F32)
    queries = jnp.where(head == 1, pltpu.roll(queries, 64, 1), queries)
    queries = jnp.where(lane < 64, queries, 0.0)
    scores = jnp.concatenate(
        [
            lax.dot_general(
                queries[8 * i : 8 * i + 8].astype(BF16),
                kv_ref[i],
                (((1,), (1,)), ((), ())),
                preferred_element_type=F32,
            )
            for i in range(pages)
        ],
        axis=0,
    ) * (64**-0.5)
    live = lane.astype(F32) < limit
    masked = jnp.where(live, scores, NEG_FILL)
    top = jnp.max(masked, axis=1, keepdims=True)
    probs = jnp.where(live, jnp.exp(masked - top), 0.0).astype(BF16).astype(F32)
    total = jnp.sum(probs, axis=1, keepdims=True)
    acc = jnp.concatenate(
        [
            jnp.dot(probs[8 * i : 8 * i + 8].astype(BF16), kv_ref[i], preferred_element_type=F32)
            for i in range(pages)
        ],
        axis=0,
    )
    alive = limit > 0.0
    lse = jnp.where(alive, top + jnp.log(jnp.maximum(total, 1e-30)), NEG_FILL)
    acc = acc / jnp.where(alive, total, 1.0)

    eye = iota((rows, rows), 0) == iota((rows, rows), 1)
    owner_row = jnp.sum(jnp.where(eye, owner, 0.0), axis=0, keepdims=True)
    lse_row = jnp.sum(jnp.where(eye, lse, 0.0), axis=0, keepdims=True)
    head_row = iota((1, rows), 1) % 8
    group = (owner == owner_row) & (head == head_row) & (lse_row > -1e29)
    peak = jnp.max(jnp.where(group, lse_row, NEG_FILL), axis=1, keepdims=True)
    mass = jnp.sum(jnp.where(group, jnp.exp(lse_row - peak), 0.0), axis=1, keepdims=True)
    joint = peak + jnp.log(jnp.maximum(mass, 1e-30))
    acc = acc * jnp.where(alive, jnp.exp(lse - joint), 0.0)
    earlier = jnp.sum(
        jnp.where(group & (iota((rows, rows), 1) < iota((rows, rows), 0)), 1.0, 0.0),
        axis=1,
        keepdims=True,
    )
    code = jnp.where(alive & (earlier == 0.0), joint + OFFSET, 0.0)
    hi, mid, lo = split3(code)
    stats = jnp.where(
        lane == 64 + head,
        hi,
        jnp.where(lane == 67 + head, mid, jnp.where(lane == 70 + head, lo, 0.0)),
    )
    stats = jnp.where(head < 3, stats, 0.0)
    stats = pltpu.roll(stats, 3, 0) + pltpu.roll(stats, 2, 0) + pltpu.roll(stats, 1, 0)
    turned = pltpu.roll(acc, 64, 1)
    placed = jnp.where(
        head == 1,
        jnp.where(lane >= 64, acc, 0.0),
        jnp.where(lane < 64, turned, 0.0),
    )
    placed = jnp.where(head == 3, stats, placed)
    placed_hi = placed.astype(BF16)
    placed_lo = (placed - placed_hi.astype(F32)).astype(BF16)
    out_row = iota((npg * 8, rows), 0)
    request = ((out_row // 8) * 4 + out_row % 4).astype(F32)
    half = (out_row // 4) % 2
    head_all = iota((npg * 8, rows), 1) % 8
    scatter = (request == owner_row) & (head_all // 2 == half)
    scattered = jnp.dot(
        scatter.astype(BF16),
        jnp.concatenate([placed_hi, placed_lo], axis=1),
        preferred_element_type=F32,
    )
    part[...] = (scattered[:, :128] + scattered[:, 128:]).astype(BF16).reshape(part.shape)

    def py_copy(src_y, dst_y):
        return remote(
            part.at[dst_y], ybuf.at[src_y], s_py.at[dst_y], r_py.at[src_y], {"pg": dst_y * nz + zz}
        )

    for d in range(1, ny):
        py_copy(yy, y_peer(d)).start()
    ybuf[yy] = part[yy]
    for d in range(1, ny):
        py_copy(y_peer(d), yy).wait_recv()
    acc_y, lse_y = merge(ybuf[...].reshape(ny, nz * 8, 128))
    zsend[...] = encode(acc_y, lse_y).reshape(zsend.shape)

    def pz_copy(src_z, dst_z):
        return remote(
            zsend.at[dst_z], zbuf.at[src_z], s_pz.at[dst_z], r_pz.at[src_z], {"pg": yy * nz + dst_z}
        )

    def pz_start(d, c):
        pz_copy(zz, z_peer(d)).start()
        return c

    lax.fori_loop(1, nz, pz_start, 0)
    zbuf[zz] = zsend[zz]

    def pz_wait(d, c):
        pz_copy(z_peer(d), zz).wait_recv()
        return c

    lax.fori_loop(1, nz, pz_wait, 0)
    attn, _ = merge(zbuf[...])
    attn = attn.astype(BF16).astype(F32)
    sub8, lane8 = iota((8, 128), 0), iota((8, 128), 1)
    pair = jnp.where(sub8 < 4, attn, 0.0).astype(BF16)
    last = jnp.where((sub8 < 4) & (lane8 < 64), pltpu.roll(attn, 4, 0), 0.0).astype(BF16)
    dec = jnp.dot(pair, w_ref[0:128, :], preferred_element_type=F32)
    dec = dec + jnp.dot(last[:, :64], w_ref[128:192, :], preferred_element_type=F32)
    proj[0] = (head_rows + dec).astype(BF16)

    @pl.when(kk != 0)
    def _():
        rs_copy(kk, 0).start()

    slot_lane = iota((st_ref.shape[0], 128), 1)
    expert = iota((st_ref.shape[0], 128), 0).astype(F32) + 1.0
    holder = [
        jnp.sum(jnp.where(st_ref[:, j : j + 1] == slot_lane, expert, 0.0), axis=0, keepdims=True)
        - 1.0
        for j in range(2)
    ]
    ids = ids_ref[pl.ds(pl.multiple_of(8 * kk, 8), 8), :].astype(F32)
    gate = rw_ref[pl.ds(pl.multiple_of(8 * kk, 8), 8), :]
    odd = iota((8, 1), 0) % 2 == 1
    dense = jnp.zeros((8, 128), F32)
    for j in range(tops):
        flip = odd if j % 2 == 0 else jnp.logical_not(odd)
        hit = ids[:, j : j + 1] == jnp.where(flip, holder[1], holder[0])
        dense = dense + jnp.where(hit, gate[:, j : j + 1], 0.0)
    dense_hi = dense.astype(BF16).astype(F32)
    dense_lo = pltpu.roll(dense - dense_hi, 64, 1)
    blk_ref[:, width:] = jnp.where(lane8 < 64, dense_hi, dense_lo).astype(BF16)

    for d in range(1, nkv):
        res_copy(k_peer(d), kk).wait_recv()
        g_copy(k_peer(d), kk).wait_recv()
    rsbuf[kk] = proj[kk]
    for d in range(1, nkv):
        rs_copy(k_peer(d), kk).wait_recv()
    gain = to_tiles(8, [gbuf[k] for k in range(nkv)])
    residual = to_tiles(8, [resbuf[k].astype(F32) for k in range(nkv)])
    projected = rsbuf[0].astype(F32)
    for k in range(1, nkv):
        projected = projected + rsbuf[k].astype(F32)
    middle = residual + projected
    square = jnp.sum(middle * middle, axis=1, keepdims=True) / width
    mid_ref[...] = middle
    gout_ref[...] = gain[1:2]
    blk_ref[:, :width] = (middle * lax.rsqrt(square + EPSILON) * gain[0:1]).astype(BF16)

    def z_sent(d, c):
        q_copy(zz, z_peer(d)).wait_send()
        pz_copy(zz, z_peer(d)).wait_send()
        return c

    lax.fori_loop(1, nz, z_sent, 0)
    for d in range(1, ny):
        qy_copy(yy, y_peer(d)).wait_send()
        py_copy(yy, y_peer(d)).wait_send()
    for d in range(1, nkv):
        res_copy(kk, k_peer(d)).wait_send()
        g_copy(kk, k_peer(d)).wait_send()
        rs_copy(kk, k_peer(d)).wait_send()
    own_wg.wait()
    own_wd.wait()
    for d in range(1, nx):
        peer = lax.rem(xx + d, nx)
        wg_copy(xx, peer).wait_send()
        wd_copy(xx, peer).wait_send()
        wg_copy(peer, xx).wait_recv()
        wd_copy(peer, xx).wait_recv()


def expert_kernel(
    nz,
    nkv,
    blk_ref,
    mid_ref,
    gout_ref,
    wgu_all,
    wd_all,
    out_ref,
    wgu,
    wdn,
    xbuf,
    obuf,
    ybuf,
    zsend,
    zbuf,
    fsend,
    fbuf,
    l_w,
    s_w,
    r_w,
    s_xz,
    r_xz,
    s_xy,
    r_xy,
    s_oy,
    r_oy,
    s_oz,
    r_oz,
    s_f,
    r_f,
):
    ny = NY
    pg, kk = lax.axis_index("pg"), lax.axis_index("kv")
    yy, zz = pg // nz, lax.rem(pg, nz)
    cc = lax.rem(kk, 2)
    sibling = kk + 1 - 2 * cc
    width = mid_ref.shape[1]

    greet(ny, nz, nkv, yy, zz, kk)

    def z_peer(d):
        return lax.rem(zz + d, nz)

    def y_peer(d):
        return lax.rem(yy + d, ny)

    def k_peer(d):
        return lax.rem(kk + d, nkv)

    xbuf[yy, zz] = blk_ref[...]

    def xz_copy(src_z, dst_z):
        return remote(
            xbuf.at[yy, src_z],
            xbuf.at[yy, src_z],
            s_xz.at[dst_z],
            r_xz.at[src_z],
            {"pg": yy * nz + dst_z},
        )

    def xz_start(d, c):
        xz_copy(zz, z_peer(d)).start()
        return c

    lax.fori_loop(1, nz, xz_start, 0)

    own_wg = pltpu.make_async_copy(wgu_all, wgu.at[:, cc], l_w.at[0])
    own_wd = pltpu.make_async_copy(wd_all, wdn.at[cc], l_w.at[1])
    own_wg.start()
    own_wd.start()

    def w_copies(core):
        return (
            remote(wgu_all, wgu.at[:, core], s_w.at[0], r_w.at[0], {"kv": sibling}),
            remote(wd_all, wdn.at[core], s_w.at[1], r_w.at[1], {"kv": sibling}),
        )

    for copy in w_copies(cc):
        copy.start()

    def xz_wait(d, c):
        xz_copy(z_peer(d), zz).wait_recv()
        return c

    lax.fori_loop(1, nz, xz_wait, 0)

    def xy_copy(src_y, dst_y):
        return remote(
            xbuf.at[src_y], xbuf.at[src_y], s_xy.at[dst_y], r_xy.at[src_y], {"pg": dst_y * nz + zz}
        )

    for d in range(1, ny):
        xy_copy(yy, y_peer(d)).start()
    own_wg.wait()
    own_wd.wait()
    for copy in w_copies(1 - cc):
        copy.wait_recv()

    def oy_copy(src_y, dst_y):
        return remote(
            obuf.at[dst_y], ybuf.at[src_y], s_oy.at[dst_y], r_oy.at[src_y], {"pg": dst_y * nz + zz}
        )

    def experts(y):
        x = xbuf[y].reshape(nz * 8, width + 128)
        gate_up = jnp.dot(
            x[:, :width], wgu[...].reshape(width, wgu.shape[3]), preferred_element_type=F32
        )
        ff = gate_up.shape[1] // 2
        v = gate_up[:, :ff]
        hidden = (v / (1.0 + jnp.exp(-v)) * gate_up[:, ff:]).astype(BF16)
        pieces = [
            jnp.dot(hidden, wdn[k % 2, k // 2], preferred_element_type=F32) for k in range(nkv)
        ]
        produced = to_tiles(nz * 8, pieces).astype(BF16).astype(F32)
        lane = iota((nz * 8, 128), 1)
        share = jnp.where(lane % 64 == pg, x[:, width:].astype(F32), 0.0)
        share = jnp.sum(share, axis=1, keepdims=True)
        obuf[y] = (produced * share).astype(BF16).reshape(nz, 8, width)

    for d in range(ny):
        if d > 0:
            xy_copy(y_peer(d), yy).wait_recv()
        experts(y_peer(d))
        if d > 0:
            oy_copy(yy, y_peer(d)).start()
    ybuf[yy] = obuf[yy]
    for d in range(1, ny):
        oy_copy(y_peer(d), yy).wait_recv()

    def add_y(z, c):
        total = ybuf[0, z].astype(F32)
        for y in range(1, ny):
            total = total + ybuf[y, z].astype(F32)
        zsend[z] = total.astype(BF16)
        return c

    lax.fori_loop(0, nz, add_y, 0)

    def oz_copy(src_z, dst_z):
        return remote(
            zsend.at[dst_z], zbuf.at[src_z], s_oz.at[dst_z], r_oz.at[src_z], {"pg": yy * nz + dst_z}
        )

    def oz_start(d, c):
        oz_copy(zz, z_peer(d)).start()
        return c

    lax.fori_loop(1, nz, oz_start, 0)
    zbuf[zz] = zsend[zz]

    def oz_wait(d, c):
        oz_copy(z_peer(d), zz).wait_recv()
        return c

    lax.fori_loop(1, nz, oz_wait, 0)
    mixed = mid_ref[...]
    for z in range(nz):
        mixed = mixed + zbuf[z].astype(F32)
    square = jnp.sum(mixed * mixed, axis=1, keepdims=True) / width
    fsend[...] = (mixed * lax.rsqrt(square + EPSILON) * gout_ref[...]).astype(BF16)

    def f_copy(src_k, dst_k):
        start = pl.multiple_of(128 * (3 * (dst_k // 2) + lax.rem(dst_k, 2)), 128)
        return remote(
            fsend.at[:, pl.ds(start, 256)],
            fbuf.at[src_k],
            s_f.at[dst_k],
            r_f.at[src_k],
            {"kv": dst_k},
        )

    for d in range(1, nkv):
        f_copy(kk, k_peer(d)).start()
    fbuf[kk] = fsend[:, pl.ds(pl.multiple_of(128 * (3 * (kk // 2) + cc), 128), 256)]
    for d in range(1, nkv):
        f_copy(k_peer(d), kk).wait_recv()
    out_ref[...] = jnp.dot(
        fbuf[...].reshape(nkv * 8, 256), placement(cc, True), preferred_element_type=F32
    ).astype(BF16)

    def z_sent(d, c):
        xz_copy(zz, z_peer(d)).wait_send()
        oz_copy(zz, z_peer(d)).wait_send()
        return c

    lax.fori_loop(1, nz, z_sent, 0)
    for d in range(1, ny):
        xy_copy(yy, y_peer(d)).wait_send()
        oy_copy(yy, y_peer(d)).wait_send()
    for d in range(1, nkv):
        f_copy(kk, k_peer(d)).wait_send()
    for copy in w_copies(cc):
        copy.wait_send()


def dma(n):
    return pltpu.SemaphoreType.DMA((n,))


def local(
    npg,
    nkv,
    residual_in,
    queries,
    prefill_attn,
    kv_cache,
    page_table,
    lengths,
    out_weight,
    norm_gain_in,
    norm_gain_out,
    expert_ids,
    route_weight,
    slot_table,
    w_gate_up,
    w_down,
):
    nz, nx, ny = npg // NY, nkv // 2, NY
    width = out_weight.shape[1]
    ff2, ff = w_gate_up.shape[2], w_down.shape[1]
    pages = kv_cache.shape[0]
    entries = page_table.size
    vmem, hbm = pl.BlockSpec(memory_space=pltpu.VMEM), pl.BlockSpec(memory_space=pl.ANY)
    block, middle, gain_out, wgu_all, wd_all = pl.pallas_call(
        functools.partial(attention_kernel, nz, nkv),
        out_shape=(
            jax.ShapeDtypeStruct((8, width + 128), BF16),
            jax.ShapeDtypeStruct((8, width), F32),
            jax.ShapeDtypeStruct((1, width), F32),
            jax.ShapeDtypeStruct((nx, 192, ff2), BF16),
            jax.ShapeDtypeStruct((nx, ff, 256), BF16),
        ),
        in_specs=[vmem] * 12 + [hbm, vmem],
        out_specs=(vmem, vmem, vmem, hbm, hbm),
        scratch_shapes=[
            pltpu.VMEM((8, 128), F32),
            pltpu.VMEM((ny, nz, 8, 128), BF16),
            pltpu.VMEM((ny, nz, 8, 128), BF16),
            pltpu.VMEM((ny, nz, 8, 128), BF16),
            pltpu.VMEM((nz, 8, 128), BF16),
            pltpu.VMEM((nz, 8, 128), BF16),
            pltpu.VMEM((64, 192), F32),
            pltpu.VMEM((nkv, 64 // nkv, width), BF16),
            pltpu.VMEM((nkv, 64 // nkv, width), BF16),
            pltpu.VMEM((nkv, 64 // nkv, 256), BF16),
            pltpu.VMEM((nkv, 64 // nkv, 256), BF16),
            pltpu.VMEM((8, 256), F32),
            pltpu.VMEM((nkv, 8, 256), F32),
            pltpu.VMEM((ff, 256), BF16),
            dma(nz),
            dma(nz),
            dma(ny),
            dma(ny),
            dma(ny),
            dma(ny),
            dma(nz),
            dma(nz),
            dma(nkv),
            dma(nkv),
            dma(nkv),
            dma(nkv),
            dma(nkv),
            dma(nkv),
            dma(nx),
            dma(nx),
            dma(nx),
            dma(nx),
            dma(2),
        ],
        compiler_params=pltpu.CompilerParams(
            collective_id=0, has_side_effects=True, vmem_limit_bytes=48 << 20
        ),
        name="attention",
    )(
        queries,
        kv_cache.reshape(pages, kv_cache.shape[2], kv_cache.shape[3]),
        page_table.reshape(1, entries),
        jnp.repeat(lengths.astype(F32), page_table.shape[1]).reshape(1, entries),
        prefill_attn,
        out_weight,
        residual_in,
        norm_gain_in.reshape(1, -1),
        norm_gain_out.reshape(1, -1),
        expert_ids,
        route_weight,
        slot_table,
        w_gate_up,
        w_down,
    )
    return pl.pallas_call(
        functools.partial(expert_kernel, nz, nkv),
        out_shape=jax.ShapeDtypeStruct(residual_in.shape, BF16),
        in_specs=[vmem] * 3 + [hbm] * 2,
        out_specs=vmem,
        scratch_shapes=[
            pltpu.VMEM((nx, 2, 192, ff2), BF16),
            pltpu.VMEM((2, nx, ff, 256), BF16),
            pltpu.VMEM((ny, nz, 8, width + 128), BF16),
            pltpu.VMEM((ny, nz, 8, width), BF16),
            pltpu.VMEM((ny, nz, 8, width), BF16),
            pltpu.VMEM((nz, 8, width), BF16),
            pltpu.VMEM((nz, 8, width), BF16),
            pltpu.VMEM((8, width), BF16),
            pltpu.VMEM((nkv, 8, 256), BF16),
            dma(2),
            dma(2),
            dma(2),
            dma(nz),
            dma(nz),
            dma(ny),
            dma(ny),
            dma(ny),
            dma(ny),
            dma(nz),
            dma(nz),
            dma(nkv),
            dma(nkv),
        ],
        compiler_params=pltpu.CompilerParams(
            collective_id=1, has_side_effects=True, vmem_limit_bytes=48 << 20
        ),
        name="experts",
    )(block, middle, gain_out, wgu_all, wd_all)


def solution(mesh):
    in_specs = (
        P("pg", "kv"),
        P("pg", "kv"),
        P("pg", "kv"),
        P("pg", "kv", None, None),
        P(),
        P(),
        P("kv", None),
        P("kv"),
        P("kv"),
        P("pg", None),
        P("pg", None),
        P(),
        P("pg", "kv", None),
        P("pg", None, "kv"),
    )
    body = functools.partial(local, mesh.shape["pg"], mesh.shape["kv"])
    return jax.shard_map(
        body, mesh=mesh, in_specs=in_specs, out_specs=P("pg", "kv"), check_vma=False
    )
```

```python
import functools
import types
import jax
import jax.numpy as jnp
from jax import lax
from jax.experimental import pallas as pl
from jax.experimental.pallas import tpu as pltpu
from jax.sharding import PartitionSpec as P

NEG_FILL = -1e30
EPSILON = 1e-06
OFFSET = 4096.0
MESH = pl.DeviceIdType.MESH
NY = 4
F32 = jnp.float32
BF16 = jnp.bfloat16


def iota(shape, dim):
    return lax.broadcasted_iota(jnp.int32, shape, dim)


def remote(src, dst, ssem, rsem, dev):
    return pltpu.make_async_remote_copy(
        src_ref=src,
        dst_ref=dst,
        send_sem=ssem,
        recv_sem=rsem,
        device_id=dev,
        device_id_type=MESH,
    )


def greet(ny, nz, nkv, yy, zz, kk):
    barrier = pltpu.get_barrier_semaphore()

    def z_body(d, c):
        peer = yy * nz + lax.rem(zz + d, nz)
        pl.semaphore_signal(barrier, inc=1, device_id={"pg": peer}, device_id_type=MESH)
        return c

    lax.fori_loop(1, nz, z_body, 0)
    for d in range(1, ny):
        peer = lax.rem(yy + d, ny) * nz + zz
        pl.semaphore_signal(barrier, inc=1, device_id={"pg": peer}, device_id_type=MESH)
    for d in range(1, nkv):
        peer = lax.rem(kk + d, nkv)
        pl.semaphore_signal(barrier, inc=1, device_id={"kv": peer}, device_id_type=MESH)
    pl.semaphore_wait(barrier, nz - 1 + ny - 1 + nkv - 1)


def to_tiles(data):
    out = []
    for j in range(len(data) // 2):
        even, odd = data[2 * j], data[2 * j + 1]
        out.append(even[:, :128])
        out.append(even[:, 128:] + odd[:, :128])
        out.append(odd[:, 128:])
    return jnp.concatenate(out, axis=1)


def placement(parity, transposed=False):
    shape = (256, 192) if transposed else (192, 256)
    narrow, wide = (1, 0) if transposed else (0, 1)
    return (iota(shape, wide) == iota(shape, narrow) + 64 * parity).astype(BF16)


def stat_tile(x2):
    n = x2.shape[0]
    lane = iota((128, 256), 0) - 64
    head = iota((128, 256), 1) // 64
    pick = ((lane >= 0) & (lane < 9) & (lane % 3 == head) & (head < 3)).astype(BF16)
    spread = jnp.dot(x2, pick, preferred_element_type=F32)
    low = pltpu.roll(spread[:, :128], n - 4, 0)
    return jnp.where(iota((n, 128), 0) % 8 < 4, low, spread[:, 128:])


def split3(x):
    hi = x.astype(BF16).astype(F32)
    mid = (x - hi).astype(BF16).astype(F32)
    return hi, mid, x - hi - mid


def encode(acc, lse):
    n = acc.shape[0]
    sub, lane = iota((n, 128), 0) % 8, iota((n, 128), 1)
    down = pltpu.roll(lse, 4, 0)
    first = pltpu.roll(down, 64, 1)
    third = pltpu.roll(lse, 64, 1)
    which = (lane - 64) % 3
    value = jnp.where(which == 0, first, jnp.where(which == 1, down, third))
    hi, mid, lo = split3(value)
    part = (lane - 64) // 3
    stat = jnp.where(part == 0, hi, jnp.where(part == 1, mid, lo))
    is_stat = (sub >= 4) & (lane >= 64)
    return jnp.where(is_stat, jnp.where(lane < 73, stat, 0.0), acc).astype(BF16)


def merge(x):
    n, m, _ = x.shape
    flat = x.reshape(n * m, 128)
    lse = stat_tile(flat).reshape(n, m, 128)
    acc = flat.astype(F32).reshape(n, m, 128)
    top = jnp.max(lse, axis=0)
    weight = jnp.exp(lse - top[None])
    total = jnp.sum(weight, axis=0)
    return jnp.sum(weight * acc, axis=0) / total, top + jnp.log(total)


def layer_kernel(nz, nkv, names, *refs):
    s = types.SimpleNamespace(**dict(zip(names, refs)))
    ny, nx = NY, nkv // 2
    npg = ny * nz
    pg, kk = lax.axis_index("pg"), lax.axis_index("kv")
    yy, zz = pg // nz, lax.rem(pg, nz)
    xx, cc = kk // 2, lax.rem(kk, 2)
    sibling = kk + 1 - 2 * cc
    pages = s.kv.shape[0]
    rows = pages * 8
    width = s.w.shape[1]
    tops = s.ids.shape[0]
    own_req = s.q.shape[0]

    def z_peer(d):
        return lax.rem(zz + d, nz)

    def y_peer(d):
        return lax.rem(yy + d, ny)

    def k_peer(d):
        return lax.rem(kk + d, nkv)

    def at(y, z):
        return {"pg": y * nz + z}

    def loop(lo, hi, body):
        def step(i, c):
            body(i)
            return c

        lax.fori_loop(lo, hi, step, 0)

    loads = {}
    for n, name in enumerate(LOADED):
        loads[name] = pltpu.make_async_copy(
            getattr(s, name + "_in"), getattr(s, name), s.l_in.at[n]
        )
        loads[name].start()
    half = s.wgu.shape[1] // 2
    own_wg = pltpu.make_async_copy(s.wgu_in.at[0], s.wgu.at[kk], s.l_w.at[0])
    own_wd = pltpu.make_async_copy(s.wd_in.at[0], s.wd.at[kk], s.l_w.at[1])
    own_wg.start()
    own_wd.start()

    greet(ny, nz, nkv, yy, zz, kk)

    loads["q"].wait()
    q32 = s.q[...].astype(F32)
    s.qtile[...] = jnp.zeros_like(s.qtile)
    s.qtile[0:own_req, :] = q32[:, :128]
    s.qtile[4 : 4 + own_req, 0:64] = q32[:, 128:]
    s.qall[yy, zz] = s.qtile[...].astype(BF16)

    def q_copy(src_z, dst_z):
        ref = s.qall.at[yy, src_z]
        return remote(ref, ref, s.s_q.at[dst_z], s.r_q.at[src_z], at(yy, dst_z))

    loop(1, nz, lambda d: q_copy(zz, z_peer(nz - d)).start())

    def w_copies(src_g, src_d, k, n, dst_k):
        return (
            remote(src_g, s.wgu.at[k], s.s_wg.at[n], s.r_wg.at[k], {"kv": dst_k}),
            remote(src_d, s.wd.at[k], s.s_wd.at[n], s.r_wd.at[k], {"kv": dst_k}),
        )

    def block_of(d, core):
        return 2 * lax.rem(xx + d, nx) + core

    def own_copies():
        out = []
        for n, dst in enumerate((block_of(1, cc), block_of(3, cc), sibling)):
            out += w_copies(s.wgu_in.at[0], s.wd_in.at[0], kk, n, dst)
        return out

    def half_copies(d, n):
        k = block_of(d, cc)
        part = pl.ds(0 if d == 3 else half, half)
        dst = {"kv": block_of(1 if d == 3 else 3, cc)}
        h = 0 if d == 3 else 1
        return (
            remote(s.wgu.at[k, part], s.wgu.at[k, part], s.s_wg.at[n], s.r_fg.at[h], dst),
            remote(s.wd.at[k, part], s.wd.at[k, part], s.s_wd.at[n], s.r_fd.at[h], dst),
        )

    def far_arrivals():
        k = block_of(2, cc)
        out = []
        for h in range(2):
            part = pl.ds(h * half, half)
            out.append(
                remote(s.wgu.at[k, part], s.wgu.at[k, part], s.s_wg.at[7], s.r_fg.at[h], {"kv": k})
            )
            out.append(
                remote(s.wd.at[k, part], s.wd.at[k, part], s.s_wd.at[7], s.r_fd.at[h], {"kv": k})
            )
        return out

    def share_copies(d, n):
        k = block_of(d, cc)
        return w_copies(s.wgu.at[k], s.wd.at[k], k, n, sibling)

    def arrival(k):
        return w_copies(s.wgu.at[k], s.wd.at[k], k, 7, sibling)

    for copy in own_copies():
        copy.start()

    def weights_middle():
        for d, n in ((3, 3), (1, 4)):
            for copy in arrival(block_of(d, cc)):
                copy.wait_recv()
            for copy in half_copies(d, n):
                copy.start()
        for d, n in ((3, 5), (1, 6)):
            for copy in share_copies(d, n):
                copy.start()

    def weights_last():
        for copy in far_arrivals():
            copy.wait_recv()
        for copy in share_copies(2, 7):
            copy.start()
        own_wg.wait()
        own_wd.wait()
        for d in range(nx):
            for copy in arrival(block_of(d, 1 - cc)):
                copy.wait_recv()

    for name in ("res", "gi", "go", "pre", "w"):
        loads[name].wait()
    spread = placement(cc)
    s.ressend[...] = (
        jnp.dot(s.res[...], spread, preferred_element_type=F32)
        .astype(BF16)
        .reshape(s.ressend.shape)
    )
    s.gsend[...] = jnp.zeros_like(s.gsend)
    s.gsend[0:1, 0:192] = s.gi[...]
    s.gsend[1:2, 0:192] = s.go[...]
    gains = s.gsend[...]
    s.gsend[...] = jnp.where(cc == 1, pltpu.roll(gains, 64, 1), gains)

    def res_copy(src_k, dst_k):
        return remote(
            s.ressend.at[dst_k],
            s.resbuf.at[src_k],
            s.s_res.at[dst_k],
            s.r_res.at[src_k],
            {"kv": dst_k},
        )

    def g_copy(src_k, dst_k):
        return remote(s.gsend, s.gbuf.at[src_k], s.s_g.at[dst_k], s.r_g.at[src_k], {"kv": dst_k})

    for d in range(1, nkv):
        res_copy(kk, k_peer(d)).start()
        g_copy(kk, k_peer(d)).start()
    s.resbuf[kk] = s.ressend[kk]
    s.gbuf[kk] = s.gsend[...]

    s.pre_s[0:own_req, :] = jnp.zeros((own_req, s.pre_s.shape[1]), F32)
    s.pre_s[own_req:, :] = s.pre[...].astype(F32)
    done = jnp.dot(s.pre_s[...].astype(BF16), s.w[...], preferred_element_type=F32)
    s.proj[...] = done.astype(BF16).reshape(s.proj.shape)
    s.head_rows[...] = done[0:8]

    def rs_copy(src_k, dst_k):
        return remote(
            s.proj.at[dst_k], s.rsbuf.at[src_k], s.s_rs.at[dst_k], s.r_rs.at[src_k], {"kv": dst_k}
        )

    for k in range(1, nkv):

        @pl.when(kk != k)
        def _():
            rs_copy(kk, k).start()

    for name in ("ids", "rw", "st"):
        loads[name].wait()
    lane8, sub8 = iota((8, 128), 1), iota((8, 128), 0)
    s.turn[...] = jnp.full((8, 128), -1.0, F32)
    s.turn[0:2, 0 : s.st.shape[1]] = s.st[...].astype(F32)
    table = s.turn[...].T
    slot_lane = iota((128, 128), 1).astype(F32)
    expert = iota((128, 128), 0).astype(F32) + 1.0
    holder = [
        jnp.sum(jnp.where(table[:, j : j + 1] == slot_lane, expert, 0.0), axis=0, keepdims=True)
        - 1.0
        for j in range(2)
    ]
    s.turn[...] = jnp.full((8, 128), -2.0, F32)
    s.turn[0:tops, 0:64] = s.ids[...].astype(F32)
    s.ids_t[...] = s.turn[...].T
    s.turn[...] = jnp.zeros((8, 128), F32)
    s.turn[0:tops, 0:64] = s.rw[...]
    s.rw_t[...] = s.turn[...].T
    ids = s.ids_t[pl.ds(pl.multiple_of(8 * kk, 8), 8), :]
    gate = s.rw_t[pl.ds(pl.multiple_of(8 * kk, 8), 8), :]
    odd = iota((8, 1), 0) % 2 == 1
    dense = jnp.zeros((8, 128), F32)
    for j in range(tops):
        flip = odd if j % 2 == 0 else jnp.logical_not(odd)
        hit = ids[:, j : j + 1] == jnp.where(flip, holder[1], holder[0])
        dense = dense + jnp.where(hit, gate[:, j : j + 1], 0.0)
    dense_hi = dense.astype(BF16).astype(F32)
    dense_lo = pltpu.roll(dense - dense_hi, 64, 1)
    s.route[...] = jnp.where(lane8 < 64, dense_hi, dense_lo).astype(BF16)

    def xz_copy(src_z, dst_z):
        ref = s.xbuf.at[yy, src_z]
        return remote(ref, ref, s.s_xz.at[dst_z], s.r_xz.at[src_z], at(yy, dst_z))

    def xy_copy(src_y, dst_y, z):
        ref = s.xbuf.at[src_y, z]
        return remote(ref, ref, s.s_xy.at[dst_y, z], s.r_xy.at[src_y, z], at(dst_y, zz))

    def nth_z(i):
        off, sign = (i + 1) // 2, lax.rem(i, 2)
        return lax.rem(zz + sign * off + (1 - sign) * (nz - off), nz)

    def norm_and_send(near_first):
        for d in range(1, nkv):
            res_copy(k_peer(d), kk).wait_recv()
            g_copy(k_peer(d), kk).wait_recv()
        s.rsbuf[kk] = s.proj[kk]
        for d in range(1, nkv):
            rs_copy(k_peer(d), kk).wait_recv()
        gain = to_tiles([s.gbuf[k] for k in range(nkv)])
        residual = to_tiles([s.resbuf[k].astype(F32) for k in range(nkv)])
        projected = s.rsbuf[0].astype(F32)
        for k in range(1, nkv):
            projected = projected + s.rsbuf[k].astype(F32)
        middle = residual + projected
        square = jnp.sum(middle * middle, axis=1, keepdims=True) / width
        s.middle[...] = middle
        s.gain_out[...] = gain[1:2]
        normed = middle * lax.rsqrt(square + EPSILON) * gain[0:1]
        s.xbuf[yy, zz] = jnp.concatenate([normed.astype(BF16), s.route[...]], axis=1)
        if near_first:
            loop(1, nz, lambda i: xz_copy(zz, nth_z(i)).start())
        else:
            loop(1, nz, lambda i: xz_copy(zz, nth_z(nz - i)).start())

    def forward(lo, hi):
        def body(i):
            z = nth_z(i)
            if lo > 0:
                xz_copy(z, zz).wait_recv()
            for d in (2, 1, 3):
                xy_copy(yy, y_peer(d), z).start()

        if lo == 0:
            for d in (2, 1, 3):
                xy_copy(yy, y_peer(d), zz).start()
            lo = 1
        if hi > lo:
            loop(lo, hi, body)

    cut = [1, max(1, nz // 2), nz]

    loads["pt"].wait()
    loads["len"].wait()
    page_row = iota((rows, 1), 0) // 8
    head = iota((rows, 1), 0) % 8
    wide = (rows, s.pt.shape[1])
    request_lane = iota(wide, 1).astype(F32)
    cached_lane = s.len[...].astype(F32)
    owner, limit = jnp.zeros(wide, F32), jnp.zeros(wide, F32)
    for j in range(s.pt.shape[0]):
        mine = s.pt[j : j + 1, :] == page_row + pg * pages
        owner = owner + jnp.where(mine, request_lane, 0.0)
        limit = limit + jnp.where(mine, cached_lane - 128.0 * j, 0.0)
    owner = jnp.sum(owner, axis=1, keepdims=True)
    limit = jnp.sum(limit, axis=1, keepdims=True)
    owner_pg = jnp.floor(owner * 0.25)
    wanted = 8.0 * owner_pg + (owner - 4.0 * owner_pg) + jnp.where(head == 2, 4.0, 0.0)
    select = (iota((rows, npg * 8), 1).astype(F32) == wanted) & (head < 3)
    s.select[...] = select.astype(BF16)

    @pl.when(kk > 0)
    def _():
        norm_and_send(True)

    loop(1, nz, lambda d: q_copy(z_peer(d), zz).wait_recv())

    def qy_copy(src_y, dst_y):
        ref = s.qall.at[src_y]
        return remote(ref, ref, s.s_qy.at[dst_y], s.r_qy.at[src_y], at(dst_y, zz))

    for d in (2, 1, 3):
        qy_copy(yy, y_peer(d)).start()

    @pl.when(kk > 0)
    def _():
        forward(0, cut[0])

    loads["kv"].wait()
    for d in range(1, ny):
        qy_copy(y_peer(d), yy).wait_recv()

    lane = iota((rows, 128), 1)
    queries = jnp.dot(s.select[...], s.qall[...].reshape(npg * 8, 128), preferred_element_type=F32)
    queries = jnp.where(head == 1, pltpu.roll(queries, 64, 1), queries)
    queries = jnp.where(lane < 64, queries, 0.0)
    scores = jnp.concatenate(
        [
            lax.dot_general(
                queries[8 * i : 8 * i + 8].astype(BF16),
                s.kv[i],
                (((1,), (1,)), ((), ())),
                preferred_element_type=F32,
            )
            for i in range(pages)
        ],
        axis=0,
    ) * (64**-0.5)
    live = lane.astype(F32) < limit
    masked = jnp.where(live, scores, NEG_FILL)
    top = jnp.max(masked, axis=1, keepdims=True)
    probs = jnp.where(live, jnp.exp(masked - top), 0.0).astype(BF16).astype(F32)
    total = jnp.sum(probs, axis=1, keepdims=True)
    acc = jnp.concatenate(
        [
            jnp.dot(probs[8 * i : 8 * i + 8].astype(BF16), s.kv[i], preferred_element_type=F32)
            for i in range(pages)
        ],
        axis=0,
    )
    alive = limit > 0.0
    lse = jnp.where(alive, top + jnp.log(jnp.maximum(total, 1e-30)), NEG_FILL)
    acc = acc / jnp.where(alive, total, 1.0)

    eye = iota((rows, rows), 0) == iota((rows, rows), 1)
    owner_row = jnp.sum(jnp.where(eye, owner, 0.0), axis=0, keepdims=True)
    lse_row = jnp.sum(jnp.where(eye, lse, 0.0), axis=0, keepdims=True)
    head_row = iota((1, rows), 1) % 8
    group = (owner == owner_row) & (head == head_row) & (lse_row > -1e29)
    peak = jnp.max(jnp.where(group, lse_row, NEG_FILL), axis=1, keepdims=True)
    mass = jnp.sum(jnp.where(group, jnp.exp(lse_row - peak), 0.0), axis=1, keepdims=True)
    joint = peak + jnp.log(jnp.maximum(mass, 1e-30))
    acc = acc * jnp.where(alive, jnp.exp(lse - joint), 0.0)
    earlier = jnp.sum(
        jnp.where(group & (iota((rows, rows), 1) < iota((rows, rows), 0)), 1.0, 0.0),
        axis=1,
        keepdims=True,
    )
    code = jnp.where(alive & (earlier == 0.0), joint + OFFSET, 0.0)
    hi, mid, lo = split3(code)
    stats = jnp.where(
        lane == 64 + head,
        hi,
        jnp.where(lane == 67 + head, mid, jnp.where(lane == 70 + head, lo, 0.0)),
    )
    stats = jnp.where(head < 3, stats, 0.0)
    stats = pltpu.roll(stats, 3, 0) + pltpu.roll(stats, 2, 0) + pltpu.roll(stats, 1, 0)
    turned = pltpu.roll(acc, 64, 1)
    placed = jnp.where(
        head == 1,
        jnp.where(lane >= 64, acc, 0.0),
        jnp.where(lane < 64, turned, 0.0),
    )
    placed = jnp.where(head == 3, stats, placed)
    placed_hi = placed.astype(BF16)
    placed_lo = (placed - placed_hi.astype(F32)).astype(BF16)
    out_row = iota((npg * 8, rows), 0)
    request = ((out_row // 8) * 4 + out_row % 4).astype(F32)
    side = (out_row // 4) % 2
    head_all = iota((npg * 8, rows), 1) % 8
    scatter = (request == owner_row) & (head_all // 2 == side)
    scattered = jnp.dot(
        scatter.astype(BF16),
        jnp.concatenate([placed_hi, placed_lo], axis=1),
        preferred_element_type=F32,
    )
    s.part[...] = (scattered[:, :128] + scattered[:, 128:]).astype(BF16).reshape(s.part.shape)

    def py_copy(src_y, dst_y):
        return remote(
            s.part.at[dst_y], s.ybuf.at[src_y], s.s_py.at[dst_y], s.r_py.at[src_y], at(dst_y, zz)
        )

    for d in (2, 1, 3):
        py_copy(yy, y_peer(d)).start()
    s.ybuf[yy] = s.part[yy]
    weights_middle()
    for d in range(1, ny):
        py_copy(y_peer(d), yy).wait_recv()
    acc_y, lse_y = merge(s.ybuf[...].reshape(ny, nz * 8, 128))
    s.zsend[...] = encode(acc_y, lse_y).reshape(s.zsend.shape)

    def pz_copy(src_z, dst_z):
        return remote(
            s.zsend.at[dst_z], s.zbuf.at[src_z], s.s_pz.at[dst_z], s.r_pz.at[src_z], at(yy, dst_z)
        )

    loop(1, nz, lambda i: pz_copy(zz, nth_z(nz - i)).start())
    s.zbuf[zz] = s.zsend[zz]

    @pl.when(kk > 0)
    def _():
        forward(cut[0], cut[1])

    loop(1, nz, lambda d: pz_copy(z_peer(d), zz).wait_recv())
    attn, _ = merge(s.zbuf[...])
    attn = attn.astype(BF16).astype(F32)
    pair = jnp.where(sub8 < 4, attn, 0.0).astype(BF16)
    last = jnp.where((sub8 < 4) & (lane8 < 64), pltpu.roll(attn, 4, 0), 0.0).astype(BF16)
    dec = jnp.dot(pair, s.w[0:128, :], preferred_element_type=F32)
    dec = dec + jnp.dot(last[:, :64], s.w[128:192, :], preferred_element_type=F32)
    s.proj[0] = (s.head_rows[...] + dec).astype(BF16)

    @pl.when(kk != 0)
    def _():
        rs_copy(kk, 0).start()
        forward(cut[1], cut[2])

    @pl.when(kk == 0)
    def _():
        norm_and_send(False)
        forward(0, nz)

    weights_last()

    groups = min(4, nz)
    size = nz // groups
    order = sorted(range(groups), key=lambda g: -min(g, groups - g))

    def nth_group(g):
        return lax.rem(zz // size + g, groups)

    def oy_copy(src_y, dst_y, g):
        part = pl.ds(g * size, size)
        return remote(
            s.obuf.at[dst_y, part],
            s.oybuf.at[src_y, part],
            s.s_oy.at[dst_y, g],
            s.r_oy.at[src_y, g],
            at(dst_y, zz),
        )

    def experts(y):
        x = s.xbuf[y].reshape(nz * 8, width + 128)
        gate_up = jnp.dot(
            x[:, :width], s.wgu[...].reshape(width, s.wgu.shape[2]), preferred_element_type=F32
        )
        ff = gate_up.shape[1] // 2
        v = gate_up[:, :ff]
        hidden = (v / (1.0 + jnp.exp(-v)) * gate_up[:, ff:]).astype(BF16)
        produced = lax.dot_general(
            hidden,
            s.wd[...].reshape(width, ff),
            (((1,), (1,)), ((), ())),
            preferred_element_type=F32,
        )
        produced = produced.astype(BF16).astype(F32)
        share = jnp.where(iota((nz * 8, 128), 1) % 64 == pg, x[:, width:].astype(F32), 0.0)
        share = jnp.sum(share, axis=1, keepdims=True)
        s.obuf[y] = (produced * share).astype(BF16).reshape(nz, 8, width)

    for d in (0, 1, 3, 2):
        y = y_peer(d)
        if d > 0:
            loop(0, nz, lambda z: xy_copy(y, yy, z).wait_recv())
        experts(y)
        if d > 0:
            for g in order:
                oy_copy(yy, y, nth_group(g)).start()

    def oz_copy(src_z, dst_z):
        return remote(
            s.ozsend.at[dst_z], s.ozbuf.at[src_z], s.s_oz.at[dst_z], s.r_oz.at[src_z], at(yy, dst_z)
        )

    for g in order:
        first = nth_group(g) * size
        for d in range(1, ny):
            oy_copy(y_peer(d), yy, nth_group(g)).wait_recv()

        def add_y(i):
            z = first + i
            summed = s.obuf[yy, z].astype(F32)
            for d in range(1, ny):
                summed = summed + s.oybuf[y_peer(d), z].astype(F32)
            s.ozsend[z] = summed.astype(BF16)

            @pl.when(z != zz)
            def _():
                oz_copy(zz, z).start()

        loop(0, size, add_y)
    s.ozbuf[zz] = s.ozsend[zz]
    loop(1, nz, lambda d: oz_copy(z_peer(d), zz).wait_recv())
    mixed = s.middle[...]
    for z in range(nz):
        mixed = mixed + s.ozbuf[z].astype(F32)
    square = jnp.sum(mixed * mixed, axis=1, keepdims=True) / width
    s.fsend[...] = (mixed * lax.rsqrt(square + EPSILON) * s.gain_out[...]).astype(BF16)

    def f_copy(src_k, dst_k):
        start = pl.multiple_of(128 * (3 * (dst_k // 2) + lax.rem(dst_k, 2)), 128)
        return remote(
            s.fsend.at[:, pl.ds(start, 256)],
            s.fbuf.at[src_k],
            s.s_f.at[dst_k],
            s.r_f.at[src_k],
            {"kv": dst_k},
        )

    for d in range(1, nkv):
        f_copy(kk, k_peer(d)).start()
    s.fbuf[kk] = s.fsend[:, pl.ds(pl.multiple_of(128 * (3 * xx + cc), 128), 256)]

    def z_sent(d):
        peer = z_peer(d)
        q_copy(zz, peer).wait_send()
        pz_copy(zz, peer).wait_send()
        xz_copy(zz, peer).wait_send()
        oz_copy(zz, peer).wait_send()

    loop(1, nz, z_sent)
    for d in range(1, ny):
        peer = y_peer(d)
        qy_copy(yy, peer).wait_send()
        py_copy(yy, peer).wait_send()
        loop(0, nz, lambda z: xy_copy(yy, peer, z).wait_send())
        loop(0, groups, lambda g: oy_copy(yy, peer, g).wait_send())
    for d in range(1, nkv):
        peer = k_peer(d)
        res_copy(kk, peer).wait_send()
        g_copy(kk, peer).wait_send()
        rs_copy(kk, peer).wait_send()
    for copy in own_copies():
        copy.wait_send()
    for copy in half_copies(3, 3) + half_copies(1, 4):
        copy.wait_send()
    for copy in share_copies(3, 5) + share_copies(1, 6) + share_copies(2, 7):
        copy.wait_send()

    for d in range(1, nkv):
        f_copy(k_peer(d), kk).wait_recv()
    s.out_v[...] = jnp.dot(
        s.fbuf[...].reshape(nkv * 8, 256), placement(cc, True), preferred_element_type=F32
    ).astype(BF16)
    for d in range(1, nkv):
        f_copy(kk, k_peer(d)).wait_send()


INPUTS = ("res", "q", "pre", "kv", "pt", "len", "w", "gi", "go", "ids", "rw", "st", "wgu", "wd")
LOADED = ("q", "res", "gi", "go", "pre", "w", "ids", "rw", "st", "pt", "len", "kv")


def dma(*shape):
    return pltpu.SemaphoreType.DMA(shape)


def local(
    npg,
    nkv,
    residual_in,
    queries,
    prefill_attn,
    kv_cache,
    page_table,
    lengths,
    out_weight,
    norm_gain_in,
    norm_gain_out,
    expert_ids,
    route_weight,
    slot_table,
    w_gate_up,
    w_down,
):
    ny, nz = NY, npg // NY
    width = out_weight.shape[1]
    ff2, ff = w_gate_up.shape[2], w_down.shape[1]
    groups = min(4, nz)
    args = (
        residual_in,
        queries,
        prefill_attn,
        kv_cache.reshape(kv_cache.shape[0], kv_cache.shape[2], kv_cache.shape[3]),
        page_table.T,
        lengths.reshape(1, -1),
        out_weight,
        norm_gain_in.reshape(1, -1),
        norm_gain_out.reshape(1, -1),
        expert_ids.T,
        route_weight.T,
        slot_table.T,
        w_gate_up,
        w_down.swapaxes(1, 2),
    )
    by_name = dict(zip(INPUTS, args))
    V = pltpu.VMEM
    scratch = {name: V(by_name[name].shape, by_name[name].dtype) for name in LOADED}
    scratch.update(
        wgu=V((nkv, 192, ff2), BF16),
        wd=V((nkv, 192, ff), BF16),
        qtile=V((8, 128), F32),
        qall=V((ny, nz, 8, 128), BF16),
        select=V((by_name["kv"].shape[0] * 8, npg * 8), BF16),
        part=V((ny, nz, 8, 128), BF16),
        ybuf=V((ny, nz, 8, 128), BF16),
        zsend=V((nz, 8, 128), BF16),
        zbuf=V((nz, 8, 128), BF16),
        pre_s=V((64, 192), F32),
        head_rows=V((8, width), F32),
        proj=V((nkv, 8, width), BF16),
        rsbuf=V((nkv, 8, width), BF16),
        ressend=V((nkv, 8, 256), BF16),
        resbuf=V((nkv, 8, 256), BF16),
        gsend=V((8, 256), F32),
        gbuf=V((nkv, 8, 256), F32),
        turn=V((8, 128), F32),
        ids_t=V((128, 8), F32),
        rw_t=V((128, 8), F32),
        route=V((8, 128), BF16),
        middle=V((8, width), F32),
        gain_out=V((1, width), F32),
        xbuf=V((ny, nz, 8, width + 128), BF16),
        obuf=V((ny, nz, 8, width), BF16),
        oybuf=V((ny, nz, 8, width), BF16),
        ozsend=V((nz, 8, width), BF16),
        ozbuf=V((nz, 8, width), BF16),
        fsend=V((8, width), BF16),
        fbuf=V((nkv, 8, 256), BF16),
        l_in=dma(len(LOADED)),
        l_w=dma(2),
        s_wg=dma(8),
        s_wd=dma(8),
        r_wg=dma(nkv),
        r_wd=dma(nkv),
        r_fg=dma(2),
        r_fd=dma(2),
        s_xy=dma(ny, nz),
        r_xy=dma(ny, nz),
        s_oy=dma(ny, groups),
        r_oy=dma(ny, groups),
    )
    for name, n in (
        ("q", nz),
        ("pz", nz),
        ("xz", nz),
        ("oz", nz),
        ("qy", ny),
        ("py", ny),
        ("rs", nkv),
        ("res", nkv),
        ("g", nkv),
        ("f", nkv),
    ):
        scratch["s_" + name] = dma(n)
        scratch["r_" + name] = dma(n)
    names = [name + "_in" for name in INPUTS] + ["out_v"] + list(scratch)
    return pl.pallas_call(
        functools.partial(layer_kernel, nz, nkv, names),
        out_shape=jax.ShapeDtypeStruct(residual_in.shape, BF16),
        in_specs=[pl.BlockSpec(memory_space=pltpu.HBM)] * len(args),
        out_specs=pl.BlockSpec(memory_space=pltpu.VMEM),
        scratch_shapes=list(scratch.values()),
        compiler_params=pltpu.CompilerParams(
            collective_id=0, has_side_effects=True, vmem_limit_bytes=56 << 20
        ),
        name="layer",
    )(*args)


def solution(mesh):
    in_specs = (
        P("pg", "kv"),
        P("pg", "kv"),
        P("pg", "kv"),
        P("pg", "kv", None, None),
        P(),
        P(),
        P("kv", None),
        P("kv"),
        P("kv"),
        P("pg", None),
        P("pg", None),
        P(),
        P("pg", "kv", None),
        P("pg", None, "kv"),
    )
    body = functools.partial(local, mesh.shape["pg"], mesh.shape["kv"])
    return jax.shard_map(
        body, mesh=mesh, in_specs=in_specs, out_specs=P("pg", "kv"), check_vma=False
    )
```

```python
import functools
import types
import jax
import jax.numpy as jnp
from jax import lax
from jax.experimental import pallas as pl
from jax.experimental.pallas import tpu as pltpu
from jax.sharding import PartitionSpec as P

NEG_FILL = -1e30
EPSILON = 1e-06
OFFSET = 4096.0
MESH = pl.DeviceIdType.MESH
NY = 4
F32 = jnp.float32
BF16 = jnp.bfloat16


def iota(shape, dim):
    return lax.broadcasted_iota(jnp.int32, shape, dim)


def remote(src, dst, ssem, rsem, dev):
    return pltpu.make_async_remote_copy(
        src_ref=src,
        dst_ref=dst,
        send_sem=ssem,
        recv_sem=rsem,
        device_id=dev,
        device_id_type=MESH,
    )


def greet(ny, nz, nkv, yy, zz, kk):
    barrier = pltpu.get_barrier_semaphore()

    def z_body(d, c):
        peer = yy * nz + lax.rem(zz + d, nz)
        pl.semaphore_signal(barrier, inc=1, device_id={"pg": peer}, device_id_type=MESH)
        return c

    lax.fori_loop(1, nz, z_body, 0)
    for d in range(1, ny):
        peer = lax.rem(yy + d, ny) * nz + zz
        pl.semaphore_signal(barrier, inc=1, device_id={"pg": peer}, device_id_type=MESH)
    for d in range(1, nkv):
        peer = lax.rem(kk + d, nkv)
        pl.semaphore_signal(barrier, inc=1, device_id={"kv": peer}, device_id_type=MESH)
    return barrier, nz - 1 + ny - 1 + nkv - 1


def to_tiles(data):
    out = []
    for j in range(len(data) // 2):
        even, odd = data[2 * j], data[2 * j + 1]
        out.append(even[:, :128])
        out.append(even[:, 128:] + odd[:, :128])
        out.append(odd[:, 128:])
    return jnp.concatenate(out, axis=1)


def placement(parity, transposed=False):
    shape = (256, 192) if transposed else (192, 256)
    narrow, wide = (1, 0) if transposed else (0, 1)
    return (iota(shape, wide) == iota(shape, narrow) + 64 * parity).astype(BF16)


def stat_tile(x2):
    n = x2.shape[0]
    lane = iota((128, 256), 0) - 64
    head = iota((128, 256), 1) // 64
    pick = ((lane >= 0) & (lane < 9) & (lane % 3 == head) & (head < 3)).astype(BF16)
    spread = jnp.dot(x2, pick, preferred_element_type=F32)
    low = pltpu.roll(spread[:, :128], n - 4, 0)
    return jnp.where(iota((n, 128), 0) % 8 < 4, low, spread[:, 128:])


def split3(x):
    hi = x.astype(BF16).astype(F32)
    mid = (x - hi).astype(BF16).astype(F32)
    return hi, mid, x - hi - mid


def encode(acc, lse):
    n = acc.shape[0]
    sub, lane = iota((n, 128), 0) % 8, iota((n, 128), 1)
    down = pltpu.roll(lse, 4, 0)
    first = pltpu.roll(down, 64, 1)
    third = pltpu.roll(lse, 64, 1)
    which = (lane - 64) % 3
    value = jnp.where(which == 0, first, jnp.where(which == 1, down, third))
    hi, mid, lo = split3(value)
    part = (lane - 64) // 3
    stat = jnp.where(part == 0, hi, jnp.where(part == 1, mid, lo))
    is_stat = (sub >= 4) & (lane >= 64)
    return jnp.where(is_stat, jnp.where(lane < 73, stat, 0.0), acc).astype(BF16)


def merge(x):
    n, m, _ = x.shape
    flat = x.reshape(n * m, 128)
    lse = stat_tile(flat).reshape(n, m, 128)
    acc = flat.astype(F32).reshape(n, m, 128)
    top = jnp.max(lse, axis=0)
    weight = jnp.exp(lse - top[None])
    total = jnp.sum(weight, axis=0)
    return jnp.sum(weight * acc, axis=0) / total, top + jnp.log(total)


def layer_kernel(nz, nkv, names, *refs):
    s = types.SimpleNamespace(**dict(zip(names, refs)))
    ny, nx = NY, nkv // 2
    npg = ny * nz
    pg, kk = lax.axis_index("pg"), lax.axis_index("kv")
    yy, zz = pg // nz, lax.rem(pg, nz)
    xx, cc = kk // 2, lax.rem(kk, 2)
    sibling = kk + 1 - 2 * cc
    pages = s.kv.shape[0]
    rows = pages * 8
    width = s.w.shape[1]
    tops = s.ids.shape[0]
    own_req = s.q.shape[0]

    def z_peer(d):
        return lax.rem(zz + d, nz)

    def y_peer(d):
        return lax.rem(yy + d, ny)

    def k_peer(d):
        return lax.rem(kk + d, nkv)

    def at(y, z):
        return {"pg": y * nz + z}

    def loop(lo, hi, body):
        def step(i, c):
            body(i)
            return c

        lax.fori_loop(lo, hi, step, 0)

    loads = {}
    for n, name in enumerate(LOADED):
        loads[name] = pltpu.make_async_copy(
            getattr(s, name + "_in"), getattr(s, name), s.l_in.at[n]
        )
        loads[name].start()
    half = s.wgu.shape[1] // 2
    own_wg = pltpu.make_async_copy(s.wgu_in.at[0], s.wgu.at[kk], s.l_w.at[0])
    own_wd = pltpu.make_async_copy(s.wd_in.at[0], s.wd.at[kk], s.l_w.at[1])
    own_wg.start()
    own_wd.start()

    barrier, callers = greet(ny, nz, nkv, yy, zz, kk)

    loads["q"].wait()
    q32 = s.q[...].astype(F32)
    s.qtile[...] = jnp.zeros_like(s.qtile)
    s.qtile[0:own_req, :] = q32[:, :128]
    s.qtile[4 : 4 + own_req, 0:64] = q32[:, 128:]
    s.qall[yy, zz] = s.qtile[...].astype(BF16)

    def q_copy(src_z, dst_z):
        ref = s.qall.at[yy, src_z]
        return remote(ref, ref, s.s_q.at[dst_z], s.r_q.at[src_z], at(yy, dst_z))


    def w_copies(src_g, src_d, k, n, dst_k):
        return (
            remote(src_g, s.wgu.at[k], s.s_wg.at[n], s.r_wg.at[k], {"kv": dst_k}),
            remote(src_d, s.wd.at[k], s.s_wd.at[n], s.r_wd.at[k], {"kv": dst_k}),
        )

    def block_of(d, core):
        return 2 * lax.rem(xx + d, nx) + core

    def own_copies():
        out = []
        for n, dst in enumerate((block_of(1, cc), block_of(3, cc), sibling)):
            out += w_copies(s.wgu_in.at[0], s.wd_in.at[0], kk, n, dst)
        return out

    def half_copies(d, n):
        k = block_of(d, cc)
        part = pl.ds(0 if d == 3 else half, half)
        dst = {"kv": block_of(1 if d == 3 else 3, cc)}
        h = 0 if d == 3 else 1
        return (
            remote(s.wgu.at[k, part], s.wgu.at[k, part], s.s_wg.at[n], s.r_fg.at[h], dst),
            remote(s.wd.at[k, part], s.wd.at[k, part], s.s_wd.at[n], s.r_fd.at[h], dst),
        )

    def far_arrivals():
        k = block_of(2, cc)
        out = []
        for h in range(2):
            part = pl.ds(h * half, half)
            out.append(
                remote(s.wgu.at[k, part], s.wgu.at[k, part], s.s_wg.at[7], s.r_fg.at[h], {"kv": k})
            )
            out.append(
                remote(s.wd.at[k, part], s.wd.at[k, part], s.s_wd.at[7], s.r_fd.at[h], {"kv": k})
            )
        return out

    def share_copies(d, n):
        k = block_of(d, cc)
        return w_copies(s.wgu.at[k], s.wd.at[k], k, n, sibling)

    def arrival(k):
        return w_copies(s.wgu.at[k], s.wd.at[k], k, 7, sibling)

    def weights_middle():
        for d, n in ((3, 3), (1, 4)):
            for copy in arrival(block_of(d, cc)):
                copy.wait_recv()
            for copy in half_copies(d, n):
                copy.start()
        for d, n in ((3, 5), (1, 6)):
            for copy in share_copies(d, n):
                copy.start()

    def weights_last():
        for copy in far_arrivals():
            copy.wait_recv()
        for copy in share_copies(2, 7):
            copy.start()
        own_wg.wait()
        own_wd.wait()
        for d in range(nx):
            for copy in arrival(block_of(d, 1 - cc)):
                copy.wait_recv()

    for name in ("res", "gi", "go", "pre", "w"):
        loads[name].wait()
    spread = placement(cc)
    s.ressend[...] = (
        jnp.dot(s.res[...], spread, preferred_element_type=F32)
        .astype(BF16)
        .reshape(s.ressend.shape)
    )
    s.gsend[...] = jnp.zeros_like(s.gsend)
    s.gsend[0:1, 0:192] = s.gi[...]
    s.gsend[1:2, 0:192] = s.go[...]
    gains = s.gsend[...]
    s.gsend[...] = jnp.where(cc == 1, pltpu.roll(gains, 64, 1), gains)

    def res_copy(src_k, dst_k):
        return remote(
            s.ressend.at[dst_k],
            s.resbuf.at[src_k],
            s.s_res.at[dst_k],
            s.r_res.at[src_k],
            {"kv": dst_k},
        )

    def g_copy(src_k, dst_k):
        return remote(s.gsend, s.gbuf.at[src_k], s.s_g.at[dst_k], s.r_g.at[src_k], {"kv": dst_k})

    s.resbuf[kk] = s.ressend[kk]
    s.gbuf[kk] = s.gsend[...]

    s.pre_s[0:own_req, :] = jnp.zeros((own_req, s.pre_s.shape[1]), F32)
    s.pre_s[own_req:, :] = s.pre[...].astype(F32)
    done = jnp.dot(s.pre_s[...].astype(BF16), s.w[...], preferred_element_type=F32)
    s.proj[...] = done.astype(BF16).reshape(s.proj.shape)

    def rs_copy(src_k, dst_k):
        return remote(
            s.proj.at[dst_k], s.rsbuf.at[src_k], s.s_rs.at[dst_k], s.r_rs.at[src_k], {"kv": dst_k}
        )


    for name in ("ids", "rw", "st"):
        loads[name].wait()
    lane8, sub8 = iota((8, 128), 1), iota((8, 128), 0)
    s.turn[...] = jnp.full((8, 128), -1.0, F32)
    s.turn[0:2, 0 : s.st.shape[1]] = s.st[...].astype(F32)
    table = s.turn[...].T
    slot_lane = iota((128, 128), 1).astype(F32)
    expert = iota((128, 128), 0).astype(F32) + 1.0
    holder = [
        jnp.sum(jnp.where(table[:, j : j + 1] == slot_lane, expert, 0.0), axis=0, keepdims=True)
        - 1.0
        for j in range(2)
    ]
    s.turn[...] = jnp.full((8, 128), -2.0, F32)
    s.turn[0:tops, 0:64] = s.ids[...].astype(F32)
    s.ids_t[...] = s.turn[...].T
    s.turn[...] = jnp.zeros((8, 128), F32)
    s.turn[0:tops, 0:64] = s.rw[...]
    s.rw_t[...] = s.turn[...].T
    ids = s.ids_t[pl.ds(pl.multiple_of(8 * kk, 8), 8), :]
    gate = s.rw_t[pl.ds(pl.multiple_of(8 * kk, 8), 8), :]
    odd = iota((8, 1), 0) % 2 == 1
    dense = jnp.zeros((8, 128), F32)
    for j in range(tops):
        flip = odd if j % 2 == 0 else jnp.logical_not(odd)
        hit = ids[:, j : j + 1] == jnp.where(flip, holder[1], holder[0])
        dense = dense + jnp.where(hit, gate[:, j : j + 1], 0.0)
    dense_hi = dense.astype(BF16).astype(F32)
    dense_lo = pltpu.roll(dense - dense_hi, 64, 1)
    s.route[...] = jnp.where(lane8 < 64, dense_hi, dense_lo).astype(BF16)

    fold = width // 2
    groups = min(4, nz)
    size = nz // groups
    order = sorted(range(groups), key=lambda g: -min(g, groups - g))
    two_stage = nz == 16

    def nth_z(i):
        off, sign = (i + 1) // 2, lax.rem(i, 2)
        return lax.rem(zz + sign * off + (1 - sign) * (nz - off), nz)

    def nth_group(g):
        return lax.rem(zz // size + g, groups)

    def make_pass(tag, folded):
        p = types.SimpleNamespace(
            **{name: getattr(s, name + "_" + tag) for name in PASS_SCRATCH}
        )
        relayed = two_stage and not folded
        cols = fold if folded else width

        def xz_copy(src_z, dst_z, sem=None):
            ref = p.x.at[yy, src_z]
            sem = p.s_xz.at[dst_z] if sem is None else p.s_xr.at[sem]
            return remote(ref, ref, sem, p.r_xz.at[src_z], at(yy, dst_z))

        def xy_copy(src_y, dst_y, z):
            ref = p.x.at[src_y, z]
            return remote(ref, ref, p.s_xy.at[dst_y, z], p.r_xy.at[src_y, z], at(dst_y, zz))

        def oy_copy(src_y, dst_y, g):
            part = pl.ds(g * size, size)
            return remote(
                p.o.at[dst_y, part],
                p.oy.at[src_y, part],
                p.s_oy.at[dst_y, g],
                p.r_oy.at[src_y, g],
                at(dst_y, zz),
            )

        def oz_copy(src_z, dst_z):
            return remote(
                p.os.at[dst_z], p.ob.at[src_z], p.s_oz.at[dst_z], p.r_oz.at[src_z], at(yy, dst_z)
            )

        def relays(i):
            src = nth_z(i)
            hops = (-1, -2, -3) if i == 7 else (1, 2, 3, 4)
            first = 0 if i == 7 else 3
            return [
                xz_copy(src, lax.rem(zz + h + nz, nz), first + n) for n, h in enumerate(hops)
            ]

        near = 9 if relayed else nz

        def send(rows):
            p.x[yy, zz] = rows
            loop(1, near, lambda i: xz_copy(zz, nth_z(near - i)).start())

        def forward(lo, hi):
            def one(i):
                z = nth_z(i)
                xz_copy(z, zz).wait_recv()
                for d in (2, 1, 3):
                    xy_copy(yy, y_peer(d), z).start()

            if lo == 0:
                for d in (2, 1, 3):
                    xy_copy(yy, y_peer(d), zz).start()
                lo = 1
            if relayed and lo < 9 <= hi:
                for i in (7, 8):
                    xz_copy(nth_z(i), zz).wait_recv()
                    for copy in relays(i):
                        copy.start()
                loop(lo, 7, one)
                for i in (7, 8):
                    for d in (2, 1, 3):
                        xy_copy(yy, y_peer(d), nth_z(i)).start()
                lo = 9
            if hi > lo:
                loop(lo, hi, one)

        def mlp(x, share):
            gate_up = jnp.dot(
                x, s.wgu[...].reshape(width, s.wgu.shape[2]), preferred_element_type=F32
            )
            ff = gate_up.shape[1] // 2
            v = gate_up[:, :ff]
            hidden = (v / (1.0 + jnp.exp(-v)) * gate_up[:, ff:]).astype(BF16)
            produced = lax.dot_general(
                hidden,
                s.wd[...].reshape(width, ff),
                (((1,), (1,)), ((), ())),
                preferred_element_type=F32,
            )
            mine = jnp.where(iota(share.shape, 1) % 64 == pg, share, 0.0)
            return produced.astype(BF16).astype(F32) * jnp.sum(mine, axis=1, keepdims=True)

        def experts_of(y):
            x = p.x[y].reshape(nz * 8, cols + 128)
            p.o[y] = mlp(x[:, :cols], x[:, cols:].astype(F32)).astype(BF16).reshape(nz, 8, cols)

        def experts_of_pair(ya, yb):
            n = nz * 8
            xa = p.x[ya].reshape(n, cols + 128).astype(F32)
            xb = p.x[yb].reshape(n, cols + 128).astype(F32)
            first = iota((n, cols), 0) % 8 < 4
            low = jnp.where(first, xa[:, :cols], pltpu.roll(xb[:, :cols], 4, 0))
            high = jnp.where(first, pltpu.roll(xa[:, :cols], n - 4, 0), xb[:, :cols])
            share = jnp.where(first[:, :128], xa[:, cols:], pltpu.roll(xb[:, cols:], 4, 0))
            out = mlp(jnp.concatenate([low, high], axis=1).astype(BF16), share)
            low, high = out[:, :cols], out[:, cols:]
            oa = jnp.where(first, low, pltpu.roll(high, 4, 0))
            ob = jnp.where(first, pltpu.roll(low, n - 4, 0), high)
            p.o[ya] = oa.astype(BF16).reshape(nz, 8, cols)
            p.o[yb] = ob.astype(BF16).reshape(nz, 8, cols)

        def arrived(d):
            if d > 0:
                loop(0, nz, lambda z: xy_copy(y_peer(d), yy, z).wait_recv())

        def go_back(d):
            if d > 0:
                for g in order:
                    oy_copy(yy, y_peer(d), nth_group(g)).start()

        def experts():
            for pair in ((0, 1), (3, 2)):
                if folded:
                    arrived(pair[0])
                    arrived(pair[1])
                    experts_of_pair(y_peer(pair[0]), y_peer(pair[1]))
                    go_back(pair[0])
                    go_back(pair[1])
                else:
                    for d in pair:
                        arrived(d)
                        experts_of(y_peer(d))
                        go_back(d)

        def sums():
            for g in order:
                first = nth_group(g) * size
                for d in range(1, ny):
                    oy_copy(y_peer(d), yy, nth_group(g)).wait_recv()

                def add_y(i):
                    z = first + i
                    summed = p.o[yy, z].astype(F32)
                    for d in range(1, ny):
                        summed = summed + p.oy[y_peer(d), z].astype(F32)
                    p.os[z] = summed.astype(BF16)

                    @pl.when(z != zz)
                    def _():
                        oz_copy(zz, z).start()

                loop(0, size, add_y)
            p.ob[zz] = p.os[zz]

        def collect():
            loop(1, nz, lambda d: oz_copy(z_peer(d), zz).wait_recv())
            total = p.ob[0].astype(F32)
            for z in range(1, nz):
                total = total + p.ob[z].astype(F32)
            return total

        def finish():
            loop(1, near, lambda i: xz_copy(zz, nth_z(i)).wait_send())
            if relayed:
                for i in (7, 8):
                    for copy in relays(i):
                        copy.wait_send()
            for d in range(1, ny):
                peer = y_peer(d)
                loop(0, nz, lambda z: xy_copy(yy, peer, z).wait_send())
                loop(0, groups, lambda g: oy_copy(yy, peer, g).wait_send())
            loop(1, nz, lambda d: oz_copy(zz, z_peer(d)).wait_send())

        return types.SimpleNamespace(
            send=send,
            forward=forward,
            experts=experts,
            sums=sums,
            collect=collect,
            finish=finish,
        )

    full, early, late = make_pass("a", False), make_pass("b", True), make_pass("c", True)
    low4 = iota((8, fold), 0) < 4

    def folded_rows(x, first):
        low, high = x[:, :fold], x[:, fold:]
        if first == 0:
            return jnp.where(low4, low, pltpu.roll(high, 4, 0))
        return jnp.where(low4, pltpu.roll(low, 4, 0), high)

    def normed_rows(middle):
        square = jnp.sum(middle * middle, axis=1, keepdims=True) / width
        return middle * lax.rsqrt(square + EPSILON) * s.gains[0:1]

    def early_rows():
        for d in range(1, nkv):
            res_copy(k_peer(d), kk).wait_recv()
            g_copy(k_peer(d), kk).wait_recv()
        s.rsbuf[kk] = s.proj[kk]
        for d in range(1, nkv):
            rs_copy(k_peer(d), kk).wait_recv()
        s.gains[...] = to_tiles([s.gbuf[k] for k in range(nkv)])
        middle = to_tiles([s.resbuf[k].astype(F32) for k in range(nkv)])
        projected = s.rsbuf[0].astype(F32)
        for k in range(1, nkv):
            projected = projected + s.rsbuf[k].astype(F32)
        middle = middle + projected
        s.middle[...] = middle
        s.normed[...] = normed_rows(middle)

    near_half = min(9, nz)

    loads["pt"].wait()
    loads["len"].wait()
    page_row = iota((rows, 1), 0) // 8
    head = iota((rows, 1), 0) % 8
    wide = (rows, s.pt.shape[1])
    request_lane = iota(wide, 1).astype(F32)
    cached_lane = s.len[...].astype(F32)
    owner, limit = jnp.zeros(wide, F32), jnp.zeros(wide, F32)
    for j in range(s.pt.shape[0]):
        mine = s.pt[j : j + 1, :] == page_row + pg * pages
        owner = owner + jnp.where(mine, request_lane, 0.0)
        limit = limit + jnp.where(mine, cached_lane - 128.0 * j, 0.0)
    owner = jnp.sum(owner, axis=1, keepdims=True)
    limit = jnp.sum(limit, axis=1, keepdims=True)
    owner_pg = jnp.floor(owner * 0.25)
    wanted = 8.0 * owner_pg + (owner - 4.0 * owner_pg) + jnp.where(head == 2, 4.0, 0.0)
    select = (iota((rows, npg * 8), 1).astype(F32) == wanted) & (head < 3)
    s.select[...] = select.astype(BF16)

    pl.semaphore_wait(barrier, callers)
    loop(1, nz, lambda d: q_copy(zz, z_peer(nz - d)).start())
    for d in range(1, nkv):
        rs_copy(kk, k_peer(d)).start()
    for d in range(1, nkv):
        res_copy(kk, k_peer(d)).start()
        g_copy(kk, k_peer(d)).start()
    for copy in own_copies():
        copy.start()

    loop(1, nz, lambda d: q_copy(z_peer(d), zz).wait_recv())

    def qy_copy(src_y, dst_y):
        ref = s.qall.at[src_y]
        return remote(ref, ref, s.s_qy.at[dst_y], s.r_qy.at[src_y], at(dst_y, zz))

    for d in (2, 1, 3):
        qy_copy(yy, y_peer(d)).start()

    early_rows()

    @pl.when(kk > 0)
    def _():
        full.send(jnp.concatenate([s.normed[...].astype(BF16), s.route[...]], axis=1))

    @pl.when(kk == 0)
    def _():
        route = pltpu.roll(s.route[...].astype(F32), 4, 0).astype(BF16)
        rows4 = folded_rows(s.normed[...], 4).astype(BF16)
        early.send(jnp.concatenate([rows4, route], axis=1))


    loads["kv"].wait()
    for d in range(1, ny):
        qy_copy(y_peer(d), yy).wait_recv()

    lane = iota((rows, 128), 1)
    queries = jnp.dot(s.select[...], s.qall[...].reshape(npg * 8, 128), preferred_element_type=F32)
    queries = jnp.where(head == 1, pltpu.roll(queries, 64, 1), queries)
    queries = jnp.where(lane < 64, queries, 0.0)
    scores = jnp.concatenate(
        [
            lax.dot_general(
                queries[8 * i : 8 * i + 8].astype(BF16),
                s.kv[i],
                (((1,), (1,)), ((), ())),
                preferred_element_type=F32,
            )
            for i in range(pages)
        ],
        axis=0,
    ) * (64**-0.5)
    live = lane.astype(F32) < limit
    masked = jnp.where(live, scores, NEG_FILL)
    top = jnp.max(masked, axis=1, keepdims=True)
    probs = jnp.where(live, jnp.exp(masked - top), 0.0).astype(BF16).astype(F32)
    total = jnp.sum(probs, axis=1, keepdims=True)
    acc = jnp.concatenate(
        [
            jnp.dot(probs[8 * i : 8 * i + 8].astype(BF16), s.kv[i], preferred_element_type=F32)
            for i in range(pages)
        ],
        axis=0,
    )
    alive = limit > 0.0
    lse = jnp.where(alive, top + jnp.log(jnp.maximum(total, 1e-30)), NEG_FILL)
    acc = acc / jnp.where(alive, total, 1.0)

    eye = iota((rows, rows), 0) == iota((rows, rows), 1)
    owner_row = jnp.sum(jnp.where(eye, owner, 0.0), axis=0, keepdims=True)
    lse_row = jnp.sum(jnp.where(eye, lse, 0.0), axis=0, keepdims=True)
    head_row = iota((1, rows), 1) % 8
    group = (owner == owner_row) & (head == head_row) & (lse_row > -1e29)
    peak = jnp.max(jnp.where(group, lse_row, NEG_FILL), axis=1, keepdims=True)
    mass = jnp.sum(jnp.where(group, jnp.exp(lse_row - peak), 0.0), axis=1, keepdims=True)
    joint = peak + jnp.log(jnp.maximum(mass, 1e-30))
    acc = acc * jnp.where(alive, jnp.exp(lse - joint), 0.0)
    earlier = jnp.sum(
        jnp.where(group & (iota((rows, rows), 1) < iota((rows, rows), 0)), 1.0, 0.0),
        axis=1,
        keepdims=True,
    )
    code = jnp.where(alive & (earlier == 0.0), joint + OFFSET, 0.0)
    hi, mid, lo = split3(code)
    stats = jnp.where(
        lane == 64 + head,
        hi,
        jnp.where(lane == 67 + head, mid, jnp.where(lane == 70 + head, lo, 0.0)),
    )
    stats = jnp.where(head < 3, stats, 0.0)
    stats = pltpu.roll(stats, 3, 0) + pltpu.roll(stats, 2, 0) + pltpu.roll(stats, 1, 0)
    turned = pltpu.roll(acc, 64, 1)
    placed = jnp.where(
        head == 1,
        jnp.where(lane >= 64, acc, 0.0),
        jnp.where(lane < 64, turned, 0.0),
    )
    placed = jnp.where(head == 3, stats, placed)
    placed_hi = placed.astype(BF16)
    placed_lo = (placed - placed_hi.astype(F32)).astype(BF16)
    out_row = iota((npg * 8, rows), 0)
    request = ((out_row // 8) * 4 + out_row % 4).astype(F32)
    side = (out_row // 4) % 2
    head_all = iota((npg * 8, rows), 1) % 8
    scatter = (request == owner_row) & (head_all // 2 == side)
    scattered = jnp.dot(
        scatter.astype(BF16),
        jnp.concatenate([placed_hi, placed_lo], axis=1),
        preferred_element_type=F32,
    )
    s.part[...] = (scattered[:, :128] + scattered[:, 128:]).astype(BF16).reshape(s.part.shape)

    def py_copy(src_y, dst_y):
        return remote(
            s.part.at[dst_y], s.ybuf.at[src_y], s.s_py.at[dst_y], s.r_py.at[src_y], at(dst_y, zz)
        )

    for d in (2, 1, 3):
        py_copy(yy, y_peer(d)).start()
    s.ybuf[yy] = s.part[yy]

    @pl.when(kk > 0)
    def _():
        full.forward(0, near_half)

    @pl.when(kk == 0)
    def _():
        early.forward(0, 1)

    for d in range(1, ny):
        py_copy(y_peer(d), yy).wait_recv()
    acc_y, lse_y = merge(s.ybuf[...].reshape(ny, nz * 8, 128))
    s.zsend[...] = encode(acc_y, lse_y).reshape(s.zsend.shape)

    def pz_copy(src_z, dst_z):
        return remote(
            s.zsend.at[dst_z], s.zbuf.at[src_z], s.s_pz.at[dst_z], s.r_pz.at[src_z], at(yy, dst_z)
        )

    loop(1, nz, lambda i: pz_copy(zz, nth_z(nz - i)).start())
    s.zbuf[zz] = s.zsend[zz]
    weights_middle()

    @pl.when(kk > 0)
    def _():
        if nz > near_half:
            full.forward(near_half, nz)

    @pl.when(kk == 0)
    def _():
        early.forward(1, nz)

    loop(1, nz, lambda d: pz_copy(z_peer(d), zz).wait_recv())
    attn, _ = merge(s.zbuf[...])
    attn = attn.astype(BF16).astype(F32)
    pair = jnp.where(sub8 < 4, attn, 0.0).astype(BF16)
    last = jnp.where((sub8 < 4) & (lane8 < 64), pltpu.roll(attn, 4, 0), 0.0).astype(BF16)
    dec = jnp.dot(pair, s.w[0:128, :], preferred_element_type=F32)
    dec = dec + jnp.dot(last[:, :64], s.w[128:192, :], preferred_element_type=F32)
    s.decsend[...] = folded_rows(dec, 0).astype(BF16)

    def dec_copy(src_k):
        return remote(s.decsend, s.decbuf.at[src_k], s.s_dec.at[0], s.r_dec.at[src_k], {"kv": 0})

    def finished(mixed):
        square = jnp.sum(mixed * mixed, axis=1, keepdims=True) / width
        s.fsend[...] = (mixed * lax.rsqrt(square + EPSILON) * s.gains[1:2]).astype(BF16)

    @pl.when(kk != 0)
    def _():
        dec_copy(kk).start()
        weights_last()
        full.experts()
        full.sums()
        finished(s.middle[...] + full.collect())

    @pl.when(kk == 0)
    def _():
        decoded = s.decsend[...].astype(F32)
        for k in range(1, nkv):
            dec_copy(k).wait_recv()
            decoded = decoded + s.decbuf[k].astype(F32)
        spread4 = jnp.concatenate([decoded, pltpu.roll(decoded, 4, 0)], axis=1)
        middle = s.middle[...] + jnp.where(iota((8, width), 0) < 4, spread4, 0.0)
        s.middle[...] = middle
        rows4 = folded_rows(normed_rows(middle), 0).astype(BF16)
        late.send(jnp.concatenate([rows4, s.route[...]], axis=1))
        weights_last()
        early.experts()
        late.forward(0, nz)
        early.sums()
        late.experts()
        late.sums()
        first, last = late.collect(), early.collect()
        low = jnp.where(low4, first, pltpu.roll(last, 4, 0))
        high = jnp.where(low4, pltpu.roll(first, 4, 0), last)
        finished(s.middle[...] + jnp.concatenate([low, high], axis=1))

    def f_copy(src_k, dst_k):
        start = pl.multiple_of(128 * (3 * (dst_k // 2) + lax.rem(dst_k, 2)), 128)
        return remote(
            s.fsend.at[:, pl.ds(start, 256)],
            s.fbuf.at[src_k],
            s.s_f.at[dst_k],
            s.r_f.at[src_k],
            {"kv": dst_k},
        )

    for d in range(1, nkv):
        f_copy(kk, k_peer(d)).start()
    s.fbuf[kk] = s.fsend[:, pl.ds(pl.multiple_of(128 * (3 * xx + cc), 128), 256)]

    def z_sent(d):
        peer = z_peer(d)
        q_copy(zz, peer).wait_send()
        pz_copy(zz, peer).wait_send()

    loop(1, nz, z_sent)
    for d in range(1, ny):
        peer = y_peer(d)
        qy_copy(yy, peer).wait_send()
        py_copy(yy, peer).wait_send()

    @pl.when(kk != 0)
    def _():
        dec_copy(kk).wait_send()
        full.finish()

    @pl.when(kk == 0)
    def _():
        early.finish()
        late.finish()

    for d in range(1, nkv):
        peer = k_peer(d)
        res_copy(kk, peer).wait_send()
        g_copy(kk, peer).wait_send()
        rs_copy(kk, peer).wait_send()
    for copy in own_copies():
        copy.wait_send()
    for copy in half_copies(3, 3) + half_copies(1, 4):
        copy.wait_send()
    for copy in share_copies(3, 5) + share_copies(1, 6) + share_copies(2, 7):
        copy.wait_send()

    for d in range(1, nkv):
        f_copy(k_peer(d), kk).wait_recv()
    s.out_v[...] = jnp.dot(
        s.fbuf[...].reshape(nkv * 8, 256), placement(cc, True), preferred_element_type=F32
    ).astype(BF16)
    for d in range(1, nkv):
        f_copy(kk, k_peer(d)).wait_send()


INPUTS = ("res", "q", "pre", "kv", "pt", "len", "w", "gi", "go", "ids", "rw", "st", "wgu", "wd")
PASS_SCRATCH = (
    "x",
    "o",
    "oy",
    "os",
    "ob",
    "s_xz",
    "r_xz",
    "s_xr",
    "s_xy",
    "r_xy",
    "s_oy",
    "r_oy",
    "s_oz",
    "r_oz",
)
LOADED = ("q", "res", "gi", "go", "pre", "w", "ids", "rw", "st", "pt", "len", "kv")


def dma(*shape):
    return pltpu.SemaphoreType.DMA(shape)


def local(
    npg,
    nkv,
    residual_in,
    queries,
    prefill_attn,
    kv_cache,
    page_table,
    lengths,
    out_weight,
    norm_gain_in,
    norm_gain_out,
    expert_ids,
    route_weight,
    slot_table,
    w_gate_up,
    w_down,
):
    ny, nz = NY, npg // NY
    width = out_weight.shape[1]
    ff2, ff = w_gate_up.shape[2], w_down.shape[1]
    groups = min(4, nz)
    args = (
        residual_in,
        queries,
        prefill_attn,
        kv_cache.reshape(kv_cache.shape[0], kv_cache.shape[2], kv_cache.shape[3]),
        page_table.T,
        lengths.reshape(1, -1),
        out_weight,
        norm_gain_in.reshape(1, -1),
        norm_gain_out.reshape(1, -1),
        expert_ids.T,
        route_weight.T,
        slot_table.T,
        w_gate_up,
        w_down.swapaxes(1, 2),
    )
    by_name = dict(zip(INPUTS, args))
    V = pltpu.VMEM
    scratch = {name: V(by_name[name].shape, by_name[name].dtype) for name in LOADED}
    scratch.update(
        wgu=V((nkv, 192, ff2), BF16),
        wd=V((nkv, 192, ff), BF16),
        qtile=V((8, 128), F32),
        qall=V((ny, nz, 8, 128), BF16),
        select=V((by_name["kv"].shape[0] * 8, npg * 8), BF16),
        part=V((ny, nz, 8, 128), BF16),
        ybuf=V((ny, nz, 8, 128), BF16),
        zsend=V((nz, 8, 128), BF16),
        zbuf=V((nz, 8, 128), BF16),
        pre_s=V((64, 192), F32),
        decsend=V((8, width // 2), BF16),
        decbuf=V((nkv, 8, width // 2), BF16),
        s_dec=dma(1),
        r_dec=dma(nkv),
        proj=V((nkv, 8, width), BF16),
        rsbuf=V((nkv, 8, width), BF16),
        ressend=V((nkv, 8, 256), BF16),
        resbuf=V((nkv, 8, 256), BF16),
        gsend=V((8, 256), F32),
        gbuf=V((nkv, 8, 256), F32),
        turn=V((8, 128), F32),
        ids_t=V((128, 8), F32),
        rw_t=V((128, 8), F32),
        route=V((8, 128), BF16),
        middle=V((8, width), F32),
        gains=V((8, width), F32),
        normed=V((8, width), F32),
        fsend=V((8, width), BF16),
        fbuf=V((nkv, 8, 256), BF16),
        l_in=dma(len(LOADED)),
        l_w=dma(2),
        s_wg=dma(8),
        s_wd=dma(8),
        r_wg=dma(nkv),
        r_wd=dma(nkv),
        r_fg=dma(2),
        r_fd=dma(2),
    )
    for name, n in (
        ("q", nz),
        ("pz", nz),
        ("qy", ny),
        ("py", ny),
        ("rs", nkv),
        ("res", nkv),
        ("g", nkv),
        ("f", nkv),
    ):
        scratch["s_" + name] = dma(n)
        scratch["r_" + name] = dma(n)
    for tag, cols in (("a", width), ("b", width // 2), ("c", width // 2)):
        shapes = dict(
            x=V((ny, nz, 8, cols + 128), BF16),
            o=V((ny, nz, 8, cols), BF16),
            oy=V((ny, nz, 8, cols), BF16),
            os=V((nz, 8, cols), BF16),
            ob=V((nz, 8, cols), BF16),
            s_xz=dma(nz),
            r_xz=dma(nz),
            s_xr=dma(8),
            s_xy=dma(ny, nz),
            r_xy=dma(ny, nz),
            s_oy=dma(ny, groups),
            r_oy=dma(ny, groups),
            s_oz=dma(nz),
            r_oz=dma(nz),
        )
        scratch.update({name + "_" + tag: shape for name, shape in shapes.items()})
    names = [name + "_in" for name in INPUTS] + ["out_v"] + list(scratch)
    return pl.pallas_call(
        functools.partial(layer_kernel, nz, nkv, names),
        out_shape=jax.ShapeDtypeStruct(residual_in.shape, BF16),
        in_specs=[pl.BlockSpec(memory_space=pltpu.HBM)] * len(args),
        out_specs=pl.BlockSpec(memory_space=pltpu.VMEM),
        scratch_shapes=list(scratch.values()),
        compiler_params=pltpu.CompilerParams(
            collective_id=0, has_side_effects=True, vmem_limit_bytes=56 << 20
        ),
        name="layer",
    )(*args)


def solution(mesh):
    in_specs = (
        P("pg", "kv"),
        P("pg", "kv"),
        P("pg", "kv"),
        P("pg", "kv", None, None),
        P(),
        P(),
        P("kv", None),
        P("kv"),
        P("kv"),
        P("pg", None),
        P("pg", None),
        P(),
        P("pg", "kv", None),
        P("pg", None, "kv"),
    )
    body = functools.partial(local, mesh.shape["pg"], mesh.shape["kv"])
    return jax.shard_map(
        body, mesh=mesh, in_specs=in_specs, out_specs=P("pg", "kv"), check_vma=False
    )
```

```python
import functools
import types
import jax
import jax.numpy as jnp
from jax import lax
from jax.experimental import pallas as pl
from jax.experimental.pallas import tpu as pltpu
from jax.sharding import PartitionSpec as P

NEG_FILL = -1e30
EPSILON = 1e-06
OFFSET = 4096.0
MESH = pl.DeviceIdType.MESH
NY = 4
F32 = jnp.float32
BF16 = jnp.bfloat16


def iota(shape, dim):
    return lax.broadcasted_iota(jnp.int32, shape, dim)


def remote(src, dst, ssem, rsem, dev):
    return pltpu.make_async_remote_copy(
        src_ref=src,
        dst_ref=dst,
        send_sem=ssem,
        recv_sem=rsem,
        device_id=dev,
        device_id_type=MESH,
    )


def greet(ny, nz, nkv, yy, zz, kk):
    barrier = pltpu.get_barrier_semaphore()

    def z_body(d, c):
        peer = yy * nz + lax.rem(zz + d, nz)
        pl.semaphore_signal(barrier, inc=1, device_id={"pg": peer}, device_id_type=MESH)
        return c

    lax.fori_loop(1, nz, z_body, 0)
    for d in range(1, ny):
        peer = lax.rem(yy + d, ny) * nz + zz
        pl.semaphore_signal(barrier, inc=1, device_id={"pg": peer}, device_id_type=MESH)
    for d in range(1, nkv):
        peer = lax.rem(kk + d, nkv)
        pl.semaphore_signal(barrier, inc=1, device_id={"kv": peer}, device_id_type=MESH)
    return barrier, nz - 1 + ny - 1 + nkv - 1


def to_tiles(data):
    out = []
    for j in range(len(data) // 2):
        even, odd = data[2 * j], data[2 * j + 1]
        out.append(even[:, :128])
        out.append(even[:, 128:] + odd[:, :128])
        out.append(odd[:, 128:])
    return jnp.concatenate(out, axis=1)


def placement(parity, transposed=False):
    shape = (256, 192) if transposed else (192, 256)
    narrow, wide = (1, 0) if transposed else (0, 1)
    return (iota(shape, wide) == iota(shape, narrow) + 64 * parity).astype(BF16)


def stat_tile(x2):
    n = x2.shape[0]
    lane = iota((128, 256), 0) - 64
    head = iota((128, 256), 1) // 64
    pick = ((lane >= 0) & (lane < 9) & (lane % 3 == head) & (head < 3)).astype(BF16)
    spread = jnp.dot(x2, pick, preferred_element_type=F32)
    low = pltpu.roll(spread[:, :128], n - 4, 0)
    return jnp.where(iota((n, 128), 0) % 8 < 4, low, spread[:, 128:])


def split3(x):
    hi = x.astype(BF16).astype(F32)
    mid = (x - hi).astype(BF16).astype(F32)
    return hi, mid, x - hi - mid


def encode(acc, lse):
    n = acc.shape[0]
    sub, lane = iota((n, 128), 0) % 8, iota((n, 128), 1)
    down = pltpu.roll(lse, 4, 0)
    first = pltpu.roll(down, 64, 1)
    third = pltpu.roll(lse, 64, 1)
    which = (lane - 64) % 3
    value = jnp.where(which == 0, first, jnp.where(which == 1, down, third))
    hi, mid, lo = split3(value)
    part = (lane - 64) // 3
    stat = jnp.where(part == 0, hi, jnp.where(part == 1, mid, lo))
    is_stat = (sub >= 4) & (lane >= 64)
    return jnp.where(is_stat, jnp.where(lane < 73, stat, 0.0), acc).astype(BF16)


def merge(x):
    n, m, _ = x.shape
    flat = x.reshape(n * m, 128)
    lse = stat_tile(flat).reshape(n, m, 128)
    acc = flat.astype(F32).reshape(n, m, 128)
    top = jnp.max(lse, axis=0)
    weight = jnp.exp(lse - top[None])
    total = jnp.sum(weight, axis=0)
    return jnp.sum(weight * acc, axis=0) / total, top + jnp.log(total)


def layer_kernel(nz, nkv, names, *refs):
    s = types.SimpleNamespace(**dict(zip(names, refs)))
    ny, nx = NY, nkv // 2
    npg = ny * nz
    pg, kk = lax.axis_index("pg"), lax.axis_index("kv")
    yy, zz = pg // nz, lax.rem(pg, nz)
    xx, cc = kk // 2, lax.rem(kk, 2)
    sibling = kk + 1 - 2 * cc
    pages = s.kv.shape[0]
    rows = pages * 8
    width = s.w.shape[1]
    tops = s.ids.shape[0]
    own_req = s.q.shape[0]

    def z_peer(d):
        return lax.rem(zz + d, nz)

    def y_peer(d):
        return lax.rem(yy + d, ny)

    def k_peer(d):
        return lax.rem(kk + d, nkv)

    def at(y, z):
        return {"pg": y * nz + z}

    def loop(lo, hi, body):
        def step(i, c):
            body(i)
            return c

        lax.fori_loop(lo, hi, step, 0)

    loads = {}
    for n, name in enumerate(LOADED):
        loads[name] = pltpu.make_async_copy(
            getattr(s, name + "_in"), getattr(s, name), s.l_in.at[n]
        )
        loads[name].start()
    half = s.wgu.shape[1] // 2
    own_wg = pltpu.make_async_copy(s.wgu_in.at[0], s.wgu.at[kk], s.l_w.at[0])
    own_wd = pltpu.make_async_copy(s.wd_in.at[0], s.wd.at[kk], s.l_w.at[1])
    own_wg.start()
    own_wd.start()

    barrier, callers = greet(ny, nz, nkv, yy, zz, kk)

    loads["q"].wait()
    q32 = s.q[...].astype(F32)
    s.qtile[...] = jnp.zeros_like(s.qtile)
    s.qtile[0:own_req, :] = q32[:, :128]
    s.qtile[4 : 4 + own_req, 0:64] = q32[:, 128:]
    s.qall[yy, zz] = s.qtile[...].astype(BF16)

    def q_copy(src_z, dst_z):
        ref = s.qall.at[yy, src_z]
        return remote(ref, ref, s.s_q.at[dst_z], s.r_q.at[src_z], at(yy, dst_z))


    def w_copies(src_g, src_d, k, n, dst_k):
        return (
            remote(src_g, s.wgu.at[k], s.s_wg.at[n], s.r_wg.at[k], {"kv": dst_k}),
            remote(src_d, s.wd.at[k], s.s_wd.at[n], s.r_wd.at[k], {"kv": dst_k}),
        )

    def block_of(d, core):
        return 2 * lax.rem(xx + d, nx) + core

    def own_copies():
        out = []
        for n, dst in enumerate((block_of(1, cc), block_of(3, cc), sibling)):
            out += w_copies(s.wgu_in.at[0], s.wd_in.at[0], kk, n, dst)
        return out

    def half_copies(d, n):
        k = block_of(d, cc)
        part = pl.ds(0 if d == 3 else half, half)
        dst = {"kv": block_of(1 if d == 3 else 3, cc)}
        h = 0 if d == 3 else 1
        return (
            remote(s.wgu.at[k, part], s.wgu.at[k, part], s.s_wg.at[n], s.r_fg.at[h], dst),
            remote(s.wd.at[k, part], s.wd.at[k, part], s.s_wd.at[n], s.r_fd.at[h], dst),
        )

    def far_arrivals():
        k = block_of(2, cc)
        out = []
        for h in range(2):
            part = pl.ds(h * half, half)
            out.append(
                remote(s.wgu.at[k, part], s.wgu.at[k, part], s.s_wg.at[7], s.r_fg.at[h], {"kv": k})
            )
            out.append(
                remote(s.wd.at[k, part], s.wd.at[k, part], s.s_wd.at[7], s.r_fd.at[h], {"kv": k})
            )
        return out

    def share_copies(d, n):
        k = block_of(d, cc)
        return w_copies(s.wgu.at[k], s.wd.at[k], k, n, sibling)

    def arrival(k):
        return w_copies(s.wgu.at[k], s.wd.at[k], k, 7, sibling)

    def weights_middle():
        for d, n in ((3, 3), (1, 4)):
            for copy in arrival(block_of(d, cc)):
                copy.wait_recv()
            for copy in half_copies(d, n):
                copy.start()
        for d, n in ((3, 5), (1, 6)):
            for copy in share_copies(d, n):
                copy.start()

    def weights_last():
        for copy in far_arrivals():
            copy.wait_recv()
        for copy in share_copies(2, 7):
            copy.start()
        own_wg.wait()
        own_wd.wait()
        for d in range(nx):
            for copy in arrival(block_of(d, 1 - cc)):
                copy.wait_recv()

    for name in ("res", "gi", "go", "pre", "w"):
        loads[name].wait()
    spread = placement(cc)
    s.ressend[...] = (
        jnp.dot(s.res[...], spread, preferred_element_type=F32)
        .astype(BF16)
        .reshape(s.ressend.shape)
    )
    s.gsend[...] = jnp.zeros_like(s.gsend)
    s.gsend[0:1, 0:192] = s.gi[...]
    s.gsend[1:2, 0:192] = s.go[...]
    gains = s.gsend[...]
    s.gsend[...] = jnp.where(cc == 1, pltpu.roll(gains, 64, 1), gains)

    def res_copy(src_k, dst_k):
        return remote(
            s.ressend.at[dst_k],
            s.resbuf.at[src_k],
            s.s_res.at[dst_k],
            s.r_res.at[src_k],
            {"kv": dst_k},
        )

    def g_copy(src_k, dst_k):
        return remote(s.gsend, s.gbuf.at[src_k], s.s_g.at[dst_k], s.r_g.at[src_k], {"kv": dst_k})

    s.resbuf[kk] = s.ressend[kk]
    s.gbuf[kk] = s.gsend[...]

    s.pre_s[0:own_req, :] = jnp.zeros((own_req, s.pre_s.shape[1]), F32)
    s.pre_s[own_req:, :] = s.pre[...].astype(F32)
    done = jnp.dot(s.pre_s[...].astype(BF16), s.w[...], preferred_element_type=F32)
    s.proj[...] = done.astype(BF16).reshape(s.proj.shape)

    def rs_copy(src_k, dst_k):
        return remote(
            s.proj.at[dst_k], s.rsbuf.at[src_k], s.s_rs.at[dst_k], s.r_rs.at[src_k], {"kv": dst_k}
        )


    for name in ("ids", "rw", "st"):
        loads[name].wait()
    lane8, sub8 = iota((8, 128), 1), iota((8, 128), 0)
    s.turn[...] = jnp.full((8, 128), -1.0, F32)
    s.turn[0:2, 0 : s.st.shape[1]] = s.st[...].astype(F32)
    table = s.turn[...].T
    slot_lane = iota((128, 128), 1).astype(F32)
    expert = iota((128, 128), 0).astype(F32) + 1.0
    holder = [
        jnp.sum(jnp.where(table[:, j : j + 1] == slot_lane, expert, 0.0), axis=0, keepdims=True)
        - 1.0
        for j in range(2)
    ]
    s.turn[...] = jnp.full((8, 128), -2.0, F32)
    s.turn[0:tops, 0:64] = s.ids[...].astype(F32)
    s.ids_t[...] = s.turn[...].T
    s.turn[...] = jnp.zeros((8, 128), F32)
    s.turn[0:tops, 0:64] = s.rw[...]
    s.rw_t[...] = s.turn[...].T
    ids = s.ids_t[pl.ds(pl.multiple_of(8 * kk, 8), 8), :]
    gate = s.rw_t[pl.ds(pl.multiple_of(8 * kk, 8), 8), :]
    odd = iota((8, 1), 0) % 2 == 1
    dense = jnp.zeros((8, 128), F32)
    for j in range(tops):
        flip = odd if j % 2 == 0 else jnp.logical_not(odd)
        hit = ids[:, j : j + 1] == jnp.where(flip, holder[1], holder[0])
        dense = dense + jnp.where(hit, gate[:, j : j + 1], 0.0)
    dense_hi = dense.astype(BF16).astype(F32)
    dense_lo = pltpu.roll(dense - dense_hi, 64, 1)
    s.route[...] = jnp.where(lane8 < 64, dense_hi, dense_lo).astype(BF16)

    fold = width // 2
    groups = min(4, nz)
    size = nz // groups
    order = sorted(range(groups), key=lambda g: -min(g, groups - g))
    two_stage = nz == 16

    def nth_z(i):
        off, sign = (i + 1) // 2, lax.rem(i, 2)
        return lax.rem(zz + sign * off + (1 - sign) * (nz - off), nz)

    def nth_group(g):
        return lax.rem(zz // size + g, groups)

    def make_pass(tag, folded):
        p = types.SimpleNamespace(
            **{name: getattr(s, name + "_" + tag) for name in PASS_SCRATCH}
        )
        relayed = two_stage and not folded
        cols = fold if folded else width

        def xz_copy(src_z, dst_z, sem=None):
            ref = p.x.at[yy, src_z]
            sem = p.s_xz.at[dst_z] if sem is None else p.s_xr.at[sem]
            return remote(ref, ref, sem, p.r_xz.at[src_z], at(yy, dst_z))

        def xy_copy(src_y, dst_y, z):
            ref = p.x.at[src_y, z]
            return remote(ref, ref, p.s_xy.at[dst_y, z], p.r_xy.at[src_y, z], at(dst_y, zz))

        def oy_copy(src_y, dst_y, g):
            part = pl.ds(g * size, size)
            return remote(
                p.o.at[dst_y, part],
                p.oy.at[src_y, part],
                p.s_oy.at[dst_y, g],
                p.r_oy.at[src_y, g],
                at(dst_y, zz),
            )

        def oz_copy(src_z, dst_z):
            return remote(
                p.os.at[dst_z], p.ob.at[src_z], p.s_oz.at[dst_z], p.r_oz.at[src_z], at(yy, dst_z)
            )

        def relays(i):
            src = nth_z(i)
            hops = (-1, -2, -3) if i == 7 else (1, 2, 3, 4)
            first = 0 if i == 7 else 3
            return [
                xz_copy(src, lax.rem(zz + h + nz, nz), first + n) for n, h in enumerate(hops)
            ]

        near = 9 if relayed else nz

        def send(rows):
            p.x[yy, zz] = rows
            loop(1, near, lambda i: xz_copy(zz, nth_z(near - i)).start())

        def forward(lo, hi):
            def one(i):
                z = nth_z(i)
                xz_copy(z, zz).wait_recv()
                for d in (2, 1, 3):
                    xy_copy(yy, y_peer(d), z).start()

            if lo == 0:
                for d in (2, 1, 3):
                    xy_copy(yy, y_peer(d), zz).start()
                lo = 1
            if relayed and lo < 9 <= hi:
                for i in (7, 8):
                    xz_copy(nth_z(i), zz).wait_recv()
                    for copy in relays(i):
                        copy.start()
                loop(lo, 7, one)
                for i in (7, 8):
                    for d in (2, 1, 3):
                        xy_copy(yy, y_peer(d), nth_z(i)).start()
                lo = 9
            if hi > lo:
                loop(lo, hi, one)

        def mlp(x, share):
            gate_up = jnp.dot(
                x, s.wgu[...].reshape(width, s.wgu.shape[2]), preferred_element_type=F32
            )
            ff = gate_up.shape[1] // 2
            v = gate_up[:, :ff]
            hidden = (v / (1.0 + jnp.exp(-v)) * gate_up[:, ff:]).astype(BF16)
            produced = lax.dot_general(
                hidden,
                s.wd[...].reshape(width, ff),
                (((1,), (1,)), ((), ())),
                preferred_element_type=F32,
            )
            mine = jnp.where(iota(share.shape, 1) % 64 == pg, share, 0.0)
            return produced.astype(BF16).astype(F32) * jnp.sum(mine, axis=1, keepdims=True)

        def experts_of_both(ya, yb):
            x = jnp.concatenate([p.x[y].reshape(nz * 8, cols + 128) for y in (ya, yb)], axis=0)
            out = mlp(x[:, :cols], x[:, cols:].astype(F32)).astype(BF16)
            p.o[ya] = out[: nz * 8].reshape(nz, 8, cols)
            p.o[yb] = out[nz * 8 :].reshape(nz, 8, cols)

        def experts_of_pair(ya, yb):
            n = nz * 8
            xa = p.x[ya].reshape(n, cols + 128).astype(F32)
            xb = p.x[yb].reshape(n, cols + 128).astype(F32)
            first = iota((n, cols), 0) % 8 < 4
            low = jnp.where(first, xa[:, :cols], pltpu.roll(xb[:, :cols], 4, 0))
            high = jnp.where(first, pltpu.roll(xa[:, :cols], n - 4, 0), xb[:, :cols])
            share = jnp.where(first[:, :128], xa[:, cols:], pltpu.roll(xb[:, cols:], 4, 0))
            out = mlp(jnp.concatenate([low, high], axis=1).astype(BF16), share)
            low, high = out[:, :cols], out[:, cols:]
            oa = jnp.where(first, low, pltpu.roll(high, 4, 0))
            ob = jnp.where(first, pltpu.roll(low, n - 4, 0), high)
            p.o[ya] = oa.astype(BF16).reshape(nz, 8, cols)
            p.o[yb] = ob.astype(BF16).reshape(nz, 8, cols)

        def arrived(d):
            if d > 0:
                loop(0, nz, lambda z: xy_copy(y_peer(d), yy, z).wait_recv())

        def go_back(d):
            if d > 0:
                for g in order:
                    oy_copy(yy, y_peer(d), nth_group(g)).start()

        def experts():
            compute = experts_of_pair if folded else experts_of_both
            for pair in ((1, 3), (2, 0)):
                for d in pair:
                    arrived(d)
                compute(y_peer(pair[0]), y_peer(pair[1]))
                for d in pair:
                    go_back(d)

        def sums():
            for g in order:
                first = nth_group(g) * size
                for d in range(1, ny):
                    oy_copy(y_peer(d), yy, nth_group(g)).wait_recv()

                def add_y(i):
                    z = first + i
                    summed = p.o[yy, z].astype(F32)
                    for d in range(1, ny):
                        summed = summed + p.oy[y_peer(d), z].astype(F32)
                    p.os[z] = summed.astype(BF16)

                    @pl.when(z != zz)
                    def _():
                        oz_copy(zz, z).start()

                loop(0, size, add_y)
            p.ob[zz] = p.os[zz]

        def collect():
            loop(1, nz, lambda d: oz_copy(z_peer(d), zz).wait_recv())
            total = p.ob[0].astype(F32)
            for z in range(1, nz):
                total = total + p.ob[z].astype(F32)
            return total

        def finish():
            loop(1, near, lambda i: xz_copy(zz, nth_z(i)).wait_send())
            if relayed:
                for i in (7, 8):
                    for copy in relays(i):
                        copy.wait_send()
            for d in range(1, ny):
                peer = y_peer(d)
                loop(0, nz, lambda z: xy_copy(yy, peer, z).wait_send())
                loop(0, groups, lambda g: oy_copy(yy, peer, g).wait_send())
            loop(1, nz, lambda d: oz_copy(zz, z_peer(d)).wait_send())

        return types.SimpleNamespace(
            send=send,
            forward=forward,
            experts=experts,
            sums=sums,
            collect=collect,
            finish=finish,
        )

    full, early, late = make_pass("a", False), make_pass("b", True), make_pass("c", True)
    low4 = iota((8, fold), 0) < 4

    def folded_rows(x, first):
        low, high = x[:, :fold], x[:, fold:]
        if first == 0:
            return jnp.where(low4, low, pltpu.roll(high, 4, 0))
        return jnp.where(low4, pltpu.roll(low, 4, 0), high)

    def normed_rows(middle):
        square = jnp.sum(middle * middle, axis=1, keepdims=True) / width
        return middle * lax.rsqrt(square + EPSILON) * s.gains[0:1]

    def early_rows():
        for d in range(1, nkv):
            res_copy(k_peer(d), kk).wait_recv()
            g_copy(k_peer(d), kk).wait_recv()
        s.rsbuf[kk] = s.proj[kk]
        for d in range(1, nkv):
            rs_copy(k_peer(d), kk).wait_recv()
        s.gains[...] = to_tiles([s.gbuf[k] for k in range(nkv)])
        middle = to_tiles([s.resbuf[k].astype(F32) for k in range(nkv)])
        projected = s.rsbuf[0].astype(F32)
        for k in range(1, nkv):
            projected = projected + s.rsbuf[k].astype(F32)
        middle = middle + projected
        s.middle[...] = middle
        s.normed[...] = normed_rows(middle)

    near_half = min(9, nz)

    loads["pt"].wait()
    loads["len"].wait()
    page_row = iota((rows, 1), 0) // 8
    head = iota((rows, 1), 0) % 8
    wide = (rows, s.pt.shape[1])
    request_lane = iota(wide, 1).astype(F32)
    cached_lane = s.len[...].astype(F32)
    owner, limit = jnp.zeros(wide, F32), jnp.zeros(wide, F32)
    for j in range(s.pt.shape[0]):
        mine = s.pt[j : j + 1, :] == page_row + pg * pages
        owner = owner + jnp.where(mine, request_lane, 0.0)
        limit = limit + jnp.where(mine, cached_lane - 128.0 * j, 0.0)
    owner = jnp.sum(owner, axis=1, keepdims=True)
    limit = jnp.sum(limit, axis=1, keepdims=True)
    owner_pg = jnp.floor(owner * 0.25)
    wanted = 8.0 * owner_pg + (owner - 4.0 * owner_pg) + jnp.where(head == 2, 4.0, 0.0)
    select = (iota((rows, npg * 8), 1).astype(F32) == wanted) & (head < 3)
    s.select[...] = select.astype(BF16)
    eye = iota((rows, rows), 0) == iota((rows, rows), 1)
    owner_row = jnp.sum(jnp.where(eye, owner, 0.0), axis=0, keepdims=True)
    s.owner_row[...] = owner_row
    out_row = iota((npg * 8, rows), 0)
    request = ((out_row // 8) * 4 + out_row % 4).astype(F32)
    side = (out_row // 4) % 2
    head_all = iota((npg * 8, rows), 1) % 8
    scatter = (request == owner_row) & (head_all // 2 == side)
    s.scatter[...] = scatter.astype(BF16)

    pl.semaphore_wait(barrier, callers)
    loop(1, nz, lambda d: q_copy(zz, z_peer(nz - d)).start())
    for d in range(1, nkv):
        rs_copy(kk, k_peer(d)).start()
    for d in range(1, nkv):
        res_copy(kk, k_peer(d)).start()
        g_copy(kk, k_peer(d)).start()
    for copy in own_copies():
        copy.start()

    loop(1, nz, lambda d: q_copy(z_peer(d), zz).wait_recv())

    def qy_copy(src_y, dst_y):
        ref = s.qall.at[src_y]
        return remote(ref, ref, s.s_qy.at[dst_y], s.r_qy.at[src_y], at(dst_y, zz))

    for d in (2, 1, 3):
        qy_copy(yy, y_peer(d)).start()

    early_rows()

    @pl.when(kk > 0)
    def _():
        full.send(jnp.concatenate([s.normed[...].astype(BF16), s.route[...]], axis=1))

    @pl.when(kk == 0)
    def _():
        route = pltpu.roll(s.route[...].astype(F32), 4, 0).astype(BF16)
        rows4 = folded_rows(s.normed[...], 4).astype(BF16)
        early.send(jnp.concatenate([rows4, route], axis=1))


    loads["kv"].wait()
    for d in range(1, ny):
        qy_copy(y_peer(d), yy).wait_recv()

    lane = iota((rows, 128), 1)
    queries = jnp.dot(s.select[...], s.qall[...].reshape(npg * 8, 128), preferred_element_type=F32)
    queries = jnp.where(head == 1, pltpu.roll(queries, 64, 1), queries)
    queries = jnp.where(lane < 64, queries, 0.0)
    scores = jnp.concatenate(
        [
            lax.dot_general(
                queries[8 * i : 8 * i + 8].astype(BF16),
                s.kv[i],
                (((1,), (1,)), ((), ())),
                preferred_element_type=F32,
            )
            for i in range(pages)
        ],
        axis=0,
    ) * (64**-0.5)
    live = lane.astype(F32) < limit
    masked = jnp.where(live, scores, NEG_FILL)
    top = jnp.max(masked, axis=1, keepdims=True)
    probs = jnp.where(live, jnp.exp(masked - top), 0.0).astype(BF16).astype(F32)
    total = jnp.sum(probs, axis=1, keepdims=True)
    acc = jnp.concatenate(
        [
            jnp.dot(probs[8 * i : 8 * i + 8].astype(BF16), s.kv[i], preferred_element_type=F32)
            for i in range(pages)
        ],
        axis=0,
    )
    alive = limit > 0.0
    lse = jnp.where(alive, top + jnp.log(jnp.maximum(total, 1e-30)), NEG_FILL)
    acc = acc / jnp.where(alive, total, 1.0)

    eye = iota((rows, rows), 0) == iota((rows, rows), 1)
    owner_row = s.owner_row[...]
    lse_row = jnp.sum(jnp.where(eye, lse, 0.0), axis=0, keepdims=True)
    head_row = iota((1, rows), 1) % 8
    group = (owner == owner_row) & (head == head_row) & (lse_row > -1e29)
    peak = jnp.max(jnp.where(group, lse_row, NEG_FILL), axis=1, keepdims=True)
    mass = jnp.sum(jnp.where(group, jnp.exp(lse_row - peak), 0.0), axis=1, keepdims=True)
    joint = peak + jnp.log(jnp.maximum(mass, 1e-30))
    acc = acc * jnp.where(alive, jnp.exp(lse - joint), 0.0)
    earlier = jnp.sum(
        jnp.where(group & (iota((rows, rows), 1) < iota((rows, rows), 0)), 1.0, 0.0),
        axis=1,
        keepdims=True,
    )
    code = jnp.where(alive & (earlier == 0.0), joint + OFFSET, 0.0)
    hi, mid, lo = split3(code)
    stats = jnp.where(
        lane == 64 + head,
        hi,
        jnp.where(lane == 67 + head, mid, jnp.where(lane == 70 + head, lo, 0.0)),
    )
    stats = jnp.where(head < 3, stats, 0.0)
    stats = pltpu.roll(stats, 3, 0) + pltpu.roll(stats, 2, 0) + pltpu.roll(stats, 1, 0)
    turned = pltpu.roll(acc, 64, 1)
    placed = jnp.where(
        head == 1,
        jnp.where(lane >= 64, acc, 0.0),
        jnp.where(lane < 64, turned, 0.0),
    )
    placed = jnp.where(head == 3, stats, placed)
    placed_hi = placed.astype(BF16)
    placed_lo = (placed - placed_hi.astype(F32)).astype(BF16)
    scattered = jnp.dot(
        s.scatter[...],
        jnp.concatenate([placed_hi, placed_lo], axis=1),
        preferred_element_type=F32,
    )
    s.part[...] = (scattered[:, :128] + scattered[:, 128:]).astype(BF16).reshape(s.part.shape)

    def py_copy(src_y, dst_y):
        return remote(
            s.part.at[dst_y], s.ybuf.at[src_y], s.s_py.at[dst_y], s.r_py.at[src_y], at(dst_y, zz)
        )

    for d in (2, 1, 3):
        py_copy(yy, y_peer(d)).start()
    s.ybuf[yy] = s.part[yy]

    @pl.when(kk > 0)
    def _():
        full.forward(0, near_half)

    @pl.when(kk == 0)
    def _():
        early.forward(0, 1)

    for d in range(1, ny):
        py_copy(y_peer(d), yy).wait_recv()
    acc_y, lse_y = merge(s.ybuf[...].reshape(ny, nz * 8, 128))
    s.zsend[...] = encode(acc_y, lse_y).reshape(s.zsend.shape)

    def pz_copy(src_z, dst_z):
        return remote(
            s.zsend.at[dst_z], s.zbuf.at[src_z], s.s_pz.at[dst_z], s.r_pz.at[src_z], at(yy, dst_z)
        )

    loop(1, nz, lambda i: pz_copy(zz, nth_z(nz - i)).start())
    s.zbuf[zz] = s.zsend[zz]
    weights_middle()

    @pl.when(kk == 0)
    def _():
        early.forward(1, nz)

    loop(1, nz, lambda d: pz_copy(z_peer(d), zz).wait_recv())
    attn, _ = merge(s.zbuf[...])
    attn = attn.astype(BF16).astype(F32)
    pair = jnp.where(sub8 < 4, attn, 0.0).astype(BF16)
    last = jnp.where((sub8 < 4) & (lane8 < 64), pltpu.roll(attn, 4, 0), 0.0).astype(BF16)
    dec = jnp.dot(pair, s.w[0:128, :], preferred_element_type=F32)
    dec = dec + jnp.dot(last[:, :64], s.w[128:192, :], preferred_element_type=F32)
    s.decsend[...] = folded_rows(dec, 0).astype(BF16)

    def dec_copy(src_k):
        return remote(s.decsend, s.decbuf.at[src_k], s.s_dec.at[0], s.r_dec.at[src_k], {"kv": 0})

    def finished(mixed):
        square = jnp.sum(mixed * mixed, axis=1, keepdims=True) / width
        s.fsend[...] = (mixed * lax.rsqrt(square + EPSILON) * s.gains[1:2]).astype(BF16)

    @pl.when(kk != 0)
    def _():
        dec_copy(kk).start()
        if nz > near_half:
            full.forward(near_half, nz)
        weights_last()
        full.experts()
        full.sums()
        finished(s.middle[...] + full.collect())

    @pl.when(kk == 0)
    def _():
        decoded = s.decsend[...].astype(F32)
        for k in range(1, nkv):
            dec_copy(k).wait_recv()
            decoded = decoded + s.decbuf[k].astype(F32)
        spread4 = jnp.concatenate([decoded, pltpu.roll(decoded, 4, 0)], axis=1)
        middle = s.middle[...] + jnp.where(iota((8, width), 0) < 4, spread4, 0.0)
        s.middle[...] = middle
        rows4 = folded_rows(normed_rows(middle), 0).astype(BF16)
        late.send(jnp.concatenate([rows4, s.route[...]], axis=1))
        weights_last()
        early.experts()
        late.forward(0, nz)
        early.sums()
        late.experts()
        late.sums()
        first, last = late.collect(), early.collect()
        low = jnp.where(low4, first, pltpu.roll(last, 4, 0))
        high = jnp.where(low4, pltpu.roll(first, 4, 0), last)
        finished(s.middle[...] + jnp.concatenate([low, high], axis=1))

    def f_copy(src_k, dst_k):
        start = pl.multiple_of(128 * (3 * (dst_k // 2) + lax.rem(dst_k, 2)), 128)
        return remote(
            s.fsend.at[:, pl.ds(start, 256)],
            s.fbuf.at[src_k],
            s.s_f.at[dst_k],
            s.r_f.at[src_k],
            {"kv": dst_k},
        )

    for d in range(1, nkv):
        f_copy(kk, k_peer(d)).start()
    s.fbuf[kk] = s.fsend[:, pl.ds(pl.multiple_of(128 * (3 * xx + cc), 128), 256)]

    def z_sent(d):
        peer = z_peer(d)
        q_copy(zz, peer).wait_send()
        pz_copy(zz, peer).wait_send()

    loop(1, nz, z_sent)
    for d in range(1, ny):
        peer = y_peer(d)
        qy_copy(yy, peer).wait_send()
        py_copy(yy, peer).wait_send()

    @pl.when(kk != 0)
    def _():
        dec_copy(kk).wait_send()
        full.finish()

    @pl.when(kk == 0)
    def _():
        early.finish()
        late.finish()

    for d in range(1, nkv):
        peer = k_peer(d)
        res_copy(kk, peer).wait_send()
        g_copy(kk, peer).wait_send()
        rs_copy(kk, peer).wait_send()
    for copy in own_copies():
        copy.wait_send()
    for copy in half_copies(3, 3) + half_copies(1, 4):
        copy.wait_send()
    for copy in share_copies(3, 5) + share_copies(1, 6) + share_copies(2, 7):
        copy.wait_send()

    for d in range(1, nkv):
        f_copy(k_peer(d), kk).wait_recv()
    s.out_v[...] = jnp.dot(
        s.fbuf[...].reshape(nkv * 8, 256), placement(cc, True), preferred_element_type=F32
    ).astype(BF16)
    for d in range(1, nkv):
        f_copy(kk, k_peer(d)).wait_send()


INPUTS = ("res", "q", "pre", "kv", "pt", "len", "w", "gi", "go", "ids", "rw", "st", "wgu", "wd")
PASS_SCRATCH = (
    "x",
    "o",
    "oy",
    "os",
    "ob",
    "s_xz",
    "r_xz",
    "s_xr",
    "s_xy",
    "r_xy",
    "s_oy",
    "r_oy",
    "s_oz",
    "r_oz",
)
LOADED = ("q", "res", "gi", "go", "pre", "w", "ids", "rw", "st", "pt", "len", "kv")


def dma(*shape):
    return pltpu.SemaphoreType.DMA(shape)


def local(
    npg,
    nkv,
    residual_in,
    queries,
    prefill_attn,
    kv_cache,
    page_table,
    lengths,
    out_weight,
    norm_gain_in,
    norm_gain_out,
    expert_ids,
    route_weight,
    slot_table,
    w_gate_up,
    w_down,
):
    ny, nz = NY, npg // NY
    width = out_weight.shape[1]
    ff2, ff = w_gate_up.shape[2], w_down.shape[1]
    groups = min(4, nz)
    args = (
        residual_in,
        queries,
        prefill_attn,
        kv_cache.reshape(kv_cache.shape[0], kv_cache.shape[2], kv_cache.shape[3]),
        page_table.T,
        lengths.reshape(1, -1),
        out_weight,
        norm_gain_in.reshape(1, -1),
        norm_gain_out.reshape(1, -1),
        expert_ids.T,
        route_weight.T,
        slot_table.T,
        w_gate_up,
        w_down.swapaxes(1, 2),
    )
    by_name = dict(zip(INPUTS, args))
    V = pltpu.VMEM
    scratch = {name: V(by_name[name].shape, by_name[name].dtype) for name in LOADED}
    scratch.update(
        wgu=V((nkv, 192, ff2), BF16),
        wd=V((nkv, 192, ff), BF16),
        qtile=V((8, 128), F32),
        qall=V((ny, nz, 8, 128), BF16),
        select=V((by_name["kv"].shape[0] * 8, npg * 8), BF16),
        part=V((ny, nz, 8, 128), BF16),
        scatter=V((npg * 8, by_name["kv"].shape[0] * 8), BF16),
        owner_row=V((1, by_name["kv"].shape[0] * 8), F32),
        ybuf=V((ny, nz, 8, 128), BF16),
        zsend=V((nz, 8, 128), BF16),
        zbuf=V((nz, 8, 128), BF16),
        pre_s=V((64, 192), F32),
        decsend=V((8, width // 2), BF16),
        decbuf=V((nkv, 8, width // 2), BF16),
        s_dec=dma(1),
        r_dec=dma(nkv),
        proj=V((nkv, 8, width), BF16),
        rsbuf=V((nkv, 8, width), BF16),
        ressend=V((nkv, 8, 256), BF16),
        resbuf=V((nkv, 8, 256), BF16),
        gsend=V((8, 256), F32),
        gbuf=V((nkv, 8, 256), F32),
        turn=V((8, 128), F32),
        ids_t=V((128, 8), F32),
        rw_t=V((128, 8), F32),
        route=V((8, 128), BF16),
        middle=V((8, width), F32),
        gains=V((8, width), F32),
        normed=V((8, width), F32),
        fsend=V((8, width), BF16),
        fbuf=V((nkv, 8, 256), BF16),
        l_in=dma(len(LOADED)),
        l_w=dma(2),
        s_wg=dma(8),
        s_wd=dma(8),
        r_wg=dma(nkv),
        r_wd=dma(nkv),
        r_fg=dma(2),
        r_fd=dma(2),
    )
    for name, n in (
        ("q", nz),
        ("pz", nz),
        ("qy", ny),
        ("py", ny),
        ("rs", nkv),
        ("res", nkv),
        ("g", nkv),
        ("f", nkv),
    ):
        scratch["s_" + name] = dma(n)
        scratch["r_" + name] = dma(n)
    for tag, cols in (("a", width), ("b", width // 2), ("c", width // 2)):
        shapes = dict(
            x=V((ny, nz, 8, cols + 128), BF16),
            o=V((ny, nz, 8, cols), BF16),
            oy=V((ny, nz, 8, cols), BF16),
            os=V((nz, 8, cols), BF16),
            ob=V((nz, 8, cols), BF16),
            s_xz=dma(nz),
            r_xz=dma(nz),
            s_xr=dma(8),
            s_xy=dma(ny, nz),
            r_xy=dma(ny, nz),
            s_oy=dma(ny, groups),
            r_oy=dma(ny, groups),
            s_oz=dma(nz),
            r_oz=dma(nz),
        )
        scratch.update({name + "_" + tag: shape for name, shape in shapes.items()})
    names = [name + "_in" for name in INPUTS] + ["out_v"] + list(scratch)
    return pl.pallas_call(
        functools.partial(layer_kernel, nz, nkv, names),
        out_shape=jax.ShapeDtypeStruct(residual_in.shape, BF16),
        in_specs=[pl.BlockSpec(memory_space=pltpu.HBM)] * len(args),
        out_specs=pl.BlockSpec(memory_space=pltpu.VMEM),
        scratch_shapes=list(scratch.values()),
        compiler_params=pltpu.CompilerParams(
            collective_id=0, has_side_effects=True, vmem_limit_bytes=56 << 20
        ),
        name="layer",
    )(*args)


def solution(mesh):
    in_specs = (
        P("pg", "kv"),
        P("pg", "kv"),
        P("pg", "kv"),
        P("pg", "kv", None, None),
        P(),
        P(),
        P("kv", None),
        P("kv"),
        P("kv"),
        P("pg", None),
        P("pg", None),
        P(),
        P("pg", "kv", None),
        P("pg", None, "kv"),
    )
    body = functools.partial(local, mesh.shape["pg"], mesh.shape["kv"])
    return jax.shard_map(
        body, mesh=mesh, in_specs=in_specs, out_specs=P("pg", "kv"), check_vma=False
    )
```

```python
import functools
import types
import jax
import jax.numpy as jnp
from jax import lax
from jax.experimental import pallas as pl
from jax.experimental.pallas import tpu as pltpu
from jax.sharding import PartitionSpec as P

NEG_FILL = -1e30
EPSILON = 1e-06
OFFSET = 4096.0
MESH = pl.DeviceIdType.MESH
NY = 4
F32 = jnp.float32
BF16 = jnp.bfloat16


def iota(shape, dim):
    return lax.broadcasted_iota(jnp.int32, shape, dim)


def remote(src, dst, ssem, rsem, dev):
    return pltpu.make_async_remote_copy(
        src_ref=src,
        dst_ref=dst,
        send_sem=ssem,
        recv_sem=rsem,
        device_id=dev,
        device_id_type=MESH,
    )


def greet(ny, nz, nkv, yy, zz, kk):
    barrier = pltpu.get_barrier_semaphore()

    def z_body(d, c):
        peer = yy * nz + lax.rem(zz + d, nz)
        pl.semaphore_signal(barrier, inc=1, device_id={"pg": peer}, device_id_type=MESH)
        return c

    lax.fori_loop(1, nz, z_body, 0)
    for d in range(1, ny):
        peer = lax.rem(yy + d, ny) * nz + zz
        pl.semaphore_signal(barrier, inc=1, device_id={"pg": peer}, device_id_type=MESH)
    for d in range(1, nkv):
        peer = lax.rem(kk + d, nkv)
        pl.semaphore_signal(barrier, inc=1, device_id={"kv": peer}, device_id_type=MESH)
    return barrier, nz - 1 + ny - 1 + nkv - 1


def to_tiles(data):
    out = []
    for j in range(len(data) // 2):
        even, odd = data[2 * j], data[2 * j + 1]
        out.append(even[:, :128])
        out.append(even[:, 128:] + odd[:, :128])
        out.append(odd[:, 128:])
    return jnp.concatenate(out, axis=1)


def placement(parity, transposed=False):
    shape = (256, 192) if transposed else (192, 256)
    narrow, wide = (1, 0) if transposed else (0, 1)
    return (iota(shape, wide) == iota(shape, narrow) + 64 * parity).astype(BF16)


def stat_tile(x2):
    n = x2.shape[0]
    lane = iota((128, 256), 0) - 64
    head = iota((128, 256), 1) // 64
    pick = ((lane >= 0) & (lane < 9) & (lane % 3 == head) & (head < 3)).astype(BF16)
    spread = jnp.dot(x2, pick, preferred_element_type=F32)
    low = pltpu.roll(spread[:, :128], n - 4, 0)
    return jnp.where(iota((n, 128), 0) % 8 < 4, low, spread[:, 128:])


def split3(x):
    hi = x.astype(BF16).astype(F32)
    mid = (x - hi).astype(BF16).astype(F32)
    return hi, mid, x - hi - mid


def encode(acc, lse):
    n = acc.shape[0]
    sub, lane = iota((n, 128), 0) % 8, iota((n, 128), 1)
    down = pltpu.roll(lse, 4, 0)
    first = pltpu.roll(down, 64, 1)
    third = pltpu.roll(lse, 64, 1)
    which = (lane - 64) % 3
    value = jnp.where(which == 0, first, jnp.where(which == 1, down, third))
    hi, mid, lo = split3(value)
    part = (lane - 64) // 3
    stat = jnp.where(part == 0, hi, jnp.where(part == 1, mid, lo))
    is_stat = (sub >= 4) & (lane >= 64)
    return jnp.where(is_stat, jnp.where(lane < 73, stat, 0.0), acc).astype(BF16)


def merge(x):
    n, m, _ = x.shape
    flat = x.reshape(n * m, 128)
    lse = stat_tile(flat).reshape(n, m, 128)
    acc = flat.astype(F32).reshape(n, m, 128)
    top = jnp.max(lse, axis=0)
    weight = jnp.exp(lse - top[None])
    total = jnp.sum(weight, axis=0)
    return jnp.sum(weight * acc, axis=0) / total, top + jnp.log(total)


def layer_kernel(nz, nkv, names, *refs):
    s = types.SimpleNamespace(**dict(zip(names, refs)))
    ny, nx = NY, nkv // 2
    npg = ny * nz
    pg, kk = lax.axis_index("pg"), lax.axis_index("kv")
    yy, zz = pg // nz, lax.rem(pg, nz)
    xx, cc = kk // 2, lax.rem(kk, 2)
    sibling = kk + 1 - 2 * cc
    pages = s.kv.shape[0]
    rows = pages * 8
    width = s.w.shape[1]
    tops = s.ids.shape[0]
    own_req = s.q.shape[0]

    def z_peer(d):
        return lax.rem(zz + d, nz)

    def y_peer(d):
        return lax.rem(yy + d, ny)

    def k_peer(d):
        return lax.rem(kk + d, nkv)

    def at(y, z):
        return {"pg": y * nz + z}

    def loop(lo, hi, body):
        def step(i, c):
            body(i)
            return c

        lax.fori_loop(lo, hi, step, 0)

    loads = {}
    for n, name in enumerate(LOADED):
        loads[name] = pltpu.make_async_copy(
            getattr(s, name + "_in"), getattr(s, name), s.l_in.at[n]
        )
        loads[name].start()
    half = s.wgu.shape[1] // 2
    own_wg = pltpu.make_async_copy(s.wgu_in.at[0], s.wgu.at[kk], s.l_w.at[0])
    own_wd = pltpu.make_async_copy(s.wd_in.at[0], s.wd.at[kk], s.l_w.at[1])
    own_wg.start()
    own_wd.start()

    barrier, callers = greet(ny, nz, nkv, yy, zz, kk)

    loads["q"].wait()
    q32 = s.q[...].astype(F32)
    s.qtile[...] = jnp.zeros_like(s.qtile)
    s.qtile[0:own_req, :] = q32[:, :128]
    s.qtile[4 : 4 + own_req, 0:64] = q32[:, 128:]
    s.qall[yy, zz] = s.qtile[0:8, :].astype(BF16)

    def q_copy(src_z, dst_z):
        ref = s.qall.at[yy, src_z]
        return remote(ref, ref, s.s_q.at[dst_z], s.r_q.at[src_z], at(yy, dst_z))


    def w_copies(src_g, src_d, k, n, dst_k):
        return (
            remote(src_g, s.wgu.at[k], s.s_wg.at[n], s.r_wg.at[k], {"kv": dst_k}),
            remote(src_d, s.wd.at[k], s.s_wd.at[n], s.r_wd.at[k], {"kv": dst_k}),
        )

    def block_of(d, core):
        return 2 * lax.rem(xx + d, nx) + core

    def own_copies():
        out = []
        for n, dst in enumerate((block_of(1, cc), block_of(3, cc), sibling)):
            out += w_copies(s.wgu_in.at[0], s.wd_in.at[0], kk, n, dst)
        return out

    def half_copies(d, n):
        k = block_of(d, cc)
        part = pl.ds(0 if d == 3 else half, half)
        dst = {"kv": block_of(1 if d == 3 else 3, cc)}
        h = 0 if d == 3 else 1
        return (
            remote(s.wgu.at[k, part], s.wgu.at[k, part], s.s_wg.at[n], s.r_fg.at[h], dst),
            remote(s.wd.at[k, part], s.wd.at[k, part], s.s_wd.at[n], s.r_fd.at[h], dst),
        )

    def far_arrivals():
        k = block_of(2, cc)
        out = []
        for h in range(2):
            part = pl.ds(h * half, half)
            out.append(
                remote(s.wgu.at[k, part], s.wgu.at[k, part], s.s_wg.at[7], s.r_fg.at[h], {"kv": k})
            )
            out.append(
                remote(s.wd.at[k, part], s.wd.at[k, part], s.s_wd.at[7], s.r_fd.at[h], {"kv": k})
            )
        return out

    def share_copies(d, n):
        k = block_of(d, cc)
        return w_copies(s.wgu.at[k], s.wd.at[k], k, n, sibling)

    def arrival(k):
        return w_copies(s.wgu.at[k], s.wd.at[k], k, 7, sibling)

    def weights_middle():
        for d, n in ((3, 3), (1, 4)):
            for copy in arrival(block_of(d, cc)):
                copy.wait_recv()
            for copy in half_copies(d, n):
                copy.start()
        for d, n in ((3, 5), (1, 6)):
            for copy in share_copies(d, n):
                copy.start()

    def weights_last():
        for copy in far_arrivals():
            copy.wait_recv()
        for copy in share_copies(2, 7):
            copy.start()
        own_wg.wait()
        own_wd.wait()
        for d in range(nx):
            for copy in arrival(block_of(d, 1 - cc)):
                copy.wait_recv()

    for name in ("res", "gi", "go", "pre", "w"):
        loads[name].wait()
    spread = placement(cc)
    s.ressend[...] = (
        jnp.dot(s.res[...], spread, preferred_element_type=F32)
        .astype(BF16)
        .reshape(s.ressend.shape)
    )
    s.gtile[...] = jnp.zeros_like(s.gtile)
    s.gtile[0:1, 0:192] = s.gi[...]
    s.gtile[1:2, 0:192] = s.go[...]
    gains = s.gtile[0:8, :]
    s.gsend[...] = jnp.where(cc == 1, pltpu.roll(gains, 64, 1), gains)

    def res_copy(src_k, dst_k):
        return remote(
            s.ressend.at[dst_k],
            s.resbuf.at[src_k],
            s.s_res.at[dst_k],
            s.r_res.at[src_k],
            {"kv": dst_k},
        )

    def g_copy(src_k, dst_k):
        return remote(s.gsend, s.gbuf.at[src_k], s.s_g.at[dst_k], s.r_g.at[src_k], {"kv": dst_k})

    s.resbuf[kk] = s.ressend[kk]
    s.gbuf[kk] = s.gsend[...]

    s.pre_s[0:own_req, :] = jnp.zeros((own_req, s.pre_s.shape[1]), F32)
    s.pre_s[own_req:64, :] = s.pre[...].astype(F32)
    done = jnp.dot(s.pre_s[0:64, :].astype(BF16), s.w[...], preferred_element_type=F32)
    s.proj[...] = done.astype(BF16).reshape(s.proj.shape)

    def rs_copy(src_k, dst_k):
        return remote(
            s.proj.at[dst_k], s.rsbuf.at[src_k], s.s_rs.at[dst_k], s.r_rs.at[src_k], {"kv": dst_k}
        )


    for name in ("ids", "rw", "st"):
        loads[name].wait()
    lane8, sub8 = iota((8, 128), 1), iota((8, 128), 0)
    s.turn[...] = jnp.full((8, 128), -1.0, F32)
    s.turn[0:2, 0 : s.st.shape[1]] = s.st[...].astype(F32)
    table = s.turn[...].T
    slot_lane = iota((128, 128), 1).astype(F32)
    expert = iota((128, 128), 0).astype(F32) + 1.0
    holder = [
        jnp.sum(jnp.where(table[:, j : j + 1] == slot_lane, expert, 0.0), axis=0, keepdims=True)
        - 1.0
        for j in range(2)
    ]
    s.turn[...] = jnp.full((8, 128), -2.0, F32)
    s.turn[0:tops, 0:64] = s.ids[...].astype(F32)
    s.ids_t[...] = s.turn[...].T
    s.turn[...] = jnp.zeros((8, 128), F32)
    s.turn[0:tops, 0:64] = s.rw[...]
    s.rw_t[...] = s.turn[...].T
    ids = s.ids_t[pl.ds(pl.multiple_of(8 * kk, 8), 8), :]
    gate = s.rw_t[pl.ds(pl.multiple_of(8 * kk, 8), 8), :]
    odd = iota((8, 1), 0) % 2 == 1
    dense = jnp.zeros((8, 128), F32)
    for j in range(tops):
        flip = odd if j % 2 == 0 else jnp.logical_not(odd)
        hit = ids[:, j : j + 1] == jnp.where(flip, holder[1], holder[0])
        dense = dense + jnp.where(hit, gate[:, j : j + 1], 0.0)
    dense_hi = dense.astype(BF16).astype(F32)
    dense_lo = pltpu.roll(dense - dense_hi, 64, 1)
    s.route[...] = jnp.where(lane8 < 64, dense_hi, dense_lo).astype(BF16)

    fold = width // 2
    groups = min(4, nz)
    size = nz // groups
    order = sorted(range(groups), key=lambda g: -min(g, groups - g))
    two_stage = nz == 16

    def nth_z(i):
        off, sign = (i + 1) // 2, lax.rem(i, 2)
        return lax.rem(zz + sign * off + (1 - sign) * (nz - off), nz)

    def nth_group(g):
        return lax.rem(zz // size + g, groups)

    def make_pass(tag, folded):
        p = types.SimpleNamespace(
            **{name: getattr(s, name + "_" + tag) for name in PASS_SCRATCH}
        )
        relayed = two_stage and not folded
        cols = fold if folded else width

        def xz_copy(src_z, dst_z, sem=None):
            ref = p.x.at[yy, src_z]
            sem = p.s_xz.at[dst_z] if sem is None else p.s_xr.at[sem]
            return remote(ref, ref, sem, p.r_xz.at[src_z], at(yy, dst_z))

        def xy_copy(src_y, dst_y, z):
            ref = p.x.at[src_y, z]
            return remote(ref, ref, p.s_xy.at[dst_y, z], p.r_xy.at[src_y, z], at(dst_y, zz))

        def oy_copy(src_y, dst_y, g):
            part = pl.ds(g * size, size)
            return remote(
                p.o.at[dst_y, part],
                p.oy.at[src_y, part],
                p.s_oy.at[dst_y, g],
                p.r_oy.at[src_y, g],
                at(dst_y, zz),
            )

        def oz_copy(src_z, dst_z):
            return remote(
                p.os.at[dst_z], p.ob.at[src_z], p.s_oz.at[dst_z], p.r_oz.at[src_z], at(yy, dst_z)
            )

        def relays(i):
            src = nth_z(i)
            hops = (-1, -2, -3) if i == 7 else (1, 2, 3, 4)
            first = 0 if i == 7 else 3
            return [
                xz_copy(src, lax.rem(zz + h + nz, nz), first + n) for n, h in enumerate(hops)
            ]

        near = 9 if relayed else nz

        def send(rows):
            p.x[yy, zz] = rows
            loop(1, near, lambda i: xz_copy(zz, nth_z(near - i)).start())

        def forward(lo, hi):
            def one(i):
                z = nth_z(i)
                xz_copy(z, zz).wait_recv()
                for d in (2, 1, 3):
                    xy_copy(yy, y_peer(d), z).start()

            if lo == 0:
                for d in (2, 1, 3):
                    xy_copy(yy, y_peer(d), zz).start()
                lo = 1
            if relayed and lo < 9 <= hi:
                for i in (7, 8):
                    xz_copy(nth_z(i), zz).wait_recv()
                    for copy in relays(i):
                        copy.start()
                loop(lo, 7, one)
                for i in (7, 8):
                    for d in (2, 1, 3):
                        xy_copy(yy, y_peer(d), nth_z(i)).start()
                lo = 9
            if hi > lo:
                loop(lo, hi, one)

        def mlp(x, share):
            gate_up = jnp.dot(
                x, s.wgu[...].reshape(width, s.wgu.shape[2]), preferred_element_type=F32
            )
            ff = gate_up.shape[1] // 2
            v = gate_up[:, :ff]
            hidden = (v / (1.0 + jnp.exp(-v)) * gate_up[:, ff:]).astype(BF16)
            produced = lax.dot_general(
                hidden,
                s.wd[...].reshape(width, ff),
                (((1,), (1,)), ((), ())),
                preferred_element_type=F32,
            )
            mine = jnp.where(iota(share.shape, 1) % 64 == pg, share, 0.0)
            return produced.astype(BF16).astype(F32) * jnp.sum(mine, axis=1, keepdims=True)

        def experts_of_both(ya, yb):
            x = jnp.concatenate([p.x[y].reshape(nz * 8, cols + 128) for y in (ya, yb)], axis=0)
            out = mlp(x[:, :cols], x[:, cols:].astype(F32)).astype(BF16)
            p.o[ya] = out[: nz * 8].reshape(nz, 8, cols)
            p.o[yb] = out[nz * 8 :].reshape(nz, 8, cols)

        def experts_of_pair(ya, yb):
            n = nz * 8
            xa = p.x[ya].reshape(n, cols + 128).astype(F32)
            xb = p.x[yb].reshape(n, cols + 128).astype(F32)
            first = iota((n, cols), 0) % 8 < 4
            low = jnp.where(first, xa[:, :cols], pltpu.roll(xb[:, :cols], 4, 0))
            high = jnp.where(first, pltpu.roll(xa[:, :cols], n - 4, 0), xb[:, :cols])
            share = jnp.where(first[:, :128], xa[:, cols:], pltpu.roll(xb[:, cols:], 4, 0))
            out = mlp(jnp.concatenate([low, high], axis=1).astype(BF16), share)
            low, high = out[:, :cols], out[:, cols:]
            oa = jnp.where(first, low, pltpu.roll(high, 4, 0))
            ob = jnp.where(first, pltpu.roll(low, n - 4, 0), high)
            p.o[ya] = oa.astype(BF16).reshape(nz, 8, cols)
            p.o[yb] = ob.astype(BF16).reshape(nz, 8, cols)

        def arrived(d):
            if d > 0:
                loop(0, nz, lambda z: xy_copy(y_peer(d), yy, z).wait_recv())

        def go_back(d):
            if d > 0:
                for g in order:
                    oy_copy(yy, y_peer(d), nth_group(g)).start()

        def experts():
            compute = experts_of_pair if folded else experts_of_both
            for pair in ((1, 3), (2, 0)):
                for d in pair:
                    arrived(d)
                compute(y_peer(pair[0]), y_peer(pair[1]))
                for d in pair:
                    go_back(d)

        def sums():
            for g in order:
                first = nth_group(g) * size
                for d in range(1, ny):
                    oy_copy(y_peer(d), yy, nth_group(g)).wait_recv()

                def add_y(i):
                    z = first + i
                    summed = p.o[yy, z].astype(F32)
                    for d in range(1, ny):
                        summed = summed + p.oy[y_peer(d), z].astype(F32)
                    p.os[z] = summed.astype(BF16)

                    @pl.when(z != zz)
                    def _():
                        oz_copy(zz, z).start()

                loop(0, size, add_y)
            p.ob[zz] = p.os[zz]

        def collect():
            loop(1, nz, lambda d: oz_copy(z_peer(d), zz).wait_recv())
            total = p.ob[0].astype(F32)
            for z in range(1, nz):
                total = total + p.ob[z].astype(F32)
            return total

        def finish():
            loop(1, near, lambda i: xz_copy(zz, nth_z(i)).wait_send())
            if relayed:
                for i in (7, 8):
                    for copy in relays(i):
                        copy.wait_send()
            for d in range(1, ny):
                peer = y_peer(d)
                loop(0, nz, lambda z: xy_copy(yy, peer, z).wait_send())
                loop(0, groups, lambda g: oy_copy(yy, peer, g).wait_send())
            loop(1, nz, lambda d: oz_copy(zz, z_peer(d)).wait_send())

        return types.SimpleNamespace(
            send=send,
            forward=forward,
            experts=experts,
            sums=sums,
            collect=collect,
            finish=finish,
        )

    full, early, late = make_pass("a", False), make_pass("b", True), make_pass("c", True)
    low4 = iota((8, fold), 0) < 4

    def folded_rows(x, first):
        low, high = x[:, :fold], x[:, fold:]
        if first == 0:
            return jnp.where(low4, low, pltpu.roll(high, 4, 0))
        return jnp.where(low4, pltpu.roll(low, 4, 0), high)

    def normed_rows(middle):
        square = jnp.sum(middle * middle, axis=1, keepdims=True) / width
        return middle * lax.rsqrt(square + EPSILON) * s.gains[0:1]

    def early_rows():
        for d in range(1, nkv):
            res_copy(k_peer(d), kk).wait_recv()
            g_copy(k_peer(d), kk).wait_recv()
        s.rsbuf[kk] = s.proj[kk]
        for d in range(1, nkv):
            rs_copy(k_peer(d), kk).wait_recv()
        s.gains[...] = to_tiles([s.gbuf[k] for k in range(nkv)])
        middle = to_tiles([s.resbuf[k].astype(F32) for k in range(nkv)])
        projected = s.rsbuf[0].astype(F32)
        for k in range(1, nkv):
            projected = projected + s.rsbuf[k].astype(F32)
        middle = middle + projected
        s.middle[...] = middle
        s.normed[...] = normed_rows(middle)

    near_half = min(9, nz)

    loads["pt"].wait()
    loads["len"].wait()
    page_row = iota((rows, 1), 0) // 8
    head = iota((rows, 1), 0) % 8
    wide = (rows, s.pt.shape[1])
    request_lane = iota(wide, 1).astype(F32)
    cached_lane = s.len[...].astype(F32)
    owner, limit = jnp.zeros(wide, F32), jnp.zeros(wide, F32)
    for j in range(s.pt.shape[0]):
        mine = s.pt[...][j : j + 1, :] == page_row + pg * pages
        owner = owner + jnp.where(mine, request_lane, 0.0)
        limit = limit + jnp.where(mine, cached_lane - 128.0 * j, 0.0)
    owner = jnp.sum(owner, axis=1, keepdims=True)
    limit = jnp.sum(limit, axis=1, keepdims=True)
    owner_pg = jnp.floor(owner * 0.25)
    wanted = 8.0 * owner_pg + (owner - 4.0 * owner_pg) + jnp.where(head == 2, 4.0, 0.0)
    select = (iota((rows, npg * 8), 1).astype(F32) == wanted) & (head < 3)
    s.select[...] = select.astype(BF16)
    eye = iota((rows, rows), 0) == iota((rows, rows), 1)
    owner_row = jnp.sum(jnp.where(eye, owner, 0.0), axis=0, keepdims=True)
    s.owner_row[...] = owner_row
    out_row = iota((npg * 8, rows), 0)
    request = ((out_row // 8) * 4 + out_row % 4).astype(F32)
    side = (out_row // 4) % 2
    head_all = iota((npg * 8, rows), 1) % 8
    scatter = (request == owner_row) & (head_all // 2 == side)
    s.scatter[...] = scatter.astype(BF16)

    pl.semaphore_wait(barrier, callers)
    loop(1, nz, lambda d: q_copy(zz, z_peer(nz - d)).start())
    for d in range(1, nkv):
        rs_copy(kk, k_peer(d)).start()
    for d in range(1, nkv):
        res_copy(kk, k_peer(d)).start()
        g_copy(kk, k_peer(d)).start()
    for copy in own_copies():
        copy.start()

    loop(1, nz, lambda d: q_copy(z_peer(d), zz).wait_recv())

    def qy_copy(src_y, dst_y):
        ref = s.qall.at[src_y]
        return remote(ref, ref, s.s_qy.at[dst_y], s.r_qy.at[src_y], at(dst_y, zz))

    for d in (2, 1, 3):
        qy_copy(yy, y_peer(d)).start()

    early_rows()

    @pl.when(kk > 0)
    def _():
        full.send(jnp.concatenate([s.normed[...].astype(BF16), s.route[...]], axis=1))

    @pl.when(kk == 0)
    def _():
        route = pltpu.roll(s.route[...].astype(F32), 4, 0).astype(BF16)
        rows4 = folded_rows(s.normed[...], 4).astype(BF16)
        early.send(jnp.concatenate([rows4, route], axis=1))


    loads["kv"].wait()
    for d in range(1, ny):
        qy_copy(y_peer(d), yy).wait_recv()

    lane = iota((rows, 128), 1)
    queries = jnp.dot(s.select[...], s.qall[...].reshape(npg * 8, 128), preferred_element_type=F32)
    queries = jnp.where(head == 1, pltpu.roll(queries, 64, 1), queries)
    queries = jnp.where(lane < 64, queries, 0.0)
    scores = jnp.concatenate(
        [
            lax.dot_general(
                queries[8 * i : 8 * i + 8].astype(BF16),
                s.kv[i],
                (((1,), (1,)), ((), ())),
                preferred_element_type=F32,
            )
            for i in range(pages)
        ],
        axis=0,
    ) * (64**-0.5)
    live = lane.astype(F32) < limit
    masked = jnp.where(live, scores, NEG_FILL)
    top = jnp.max(masked, axis=1, keepdims=True)
    probs = jnp.where(live, jnp.exp(masked - top), 0.0).astype(BF16).astype(F32)
    total = jnp.sum(probs, axis=1, keepdims=True)
    acc = jnp.concatenate(
        [
            jnp.dot(probs[8 * i : 8 * i + 8].astype(BF16), s.kv[i], preferred_element_type=F32)
            for i in range(pages)
        ],
        axis=0,
    )
    alive = limit > 0.0
    lse = jnp.where(alive, top + jnp.log(jnp.maximum(total, 1e-30)), NEG_FILL)
    acc = acc / jnp.where(alive, total, 1.0)

    eye = iota((rows, rows), 0) == iota((rows, rows), 1)
    owner_row = s.owner_row[...]
    lse_row = jnp.sum(jnp.where(eye, lse, 0.0), axis=0, keepdims=True)
    head_row = iota((1, rows), 1) % 8
    group = (owner == owner_row) & (head == head_row) & (lse_row > -1e29)
    peak = jnp.max(jnp.where(group, lse_row, NEG_FILL), axis=1, keepdims=True)
    mass = jnp.sum(jnp.where(group, jnp.exp(lse_row - peak), 0.0), axis=1, keepdims=True)
    joint = peak + jnp.log(jnp.maximum(mass, 1e-30))
    acc = acc * jnp.where(alive, jnp.exp(lse - joint), 0.0)
    earlier = jnp.sum(
        jnp.where(group & (iota((rows, rows), 1) < iota((rows, rows), 0)), 1.0, 0.0),
        axis=1,
        keepdims=True,
    )
    code = jnp.where(alive & (earlier == 0.0), joint + OFFSET, 0.0)
    hi, mid, lo = split3(code)
    stats = jnp.where(
        lane == 64 + head,
        hi,
        jnp.where(lane == 67 + head, mid, jnp.where(lane == 70 + head, lo, 0.0)),
    )
    stats = jnp.where(head < 3, stats, 0.0)
    stats = pltpu.roll(stats, 3, 0) + pltpu.roll(stats, 2, 0) + pltpu.roll(stats, 1, 0)
    turned = pltpu.roll(acc, 64, 1)
    placed = jnp.where(
        head == 1,
        jnp.where(lane >= 64, acc, 0.0),
        jnp.where(lane < 64, turned, 0.0),
    )
    placed = jnp.where(head == 3, stats, placed)
    placed_hi = placed.astype(BF16)
    placed_lo = (placed - placed_hi.astype(F32)).astype(BF16)
    scattered = jnp.dot(
        s.scatter[...],
        jnp.concatenate([placed_hi, placed_lo], axis=1),
        preferred_element_type=F32,
    )
    s.part[...] = (scattered[:, :128] + scattered[:, 128:]).astype(BF16).reshape(s.part.shape)

    def py_copy(src_y, dst_y):
        return remote(
            s.part.at[dst_y], s.ybuf.at[src_y], s.s_py.at[dst_y], s.r_py.at[src_y], at(dst_y, zz)
        )

    for d in (2, 1, 3):
        py_copy(yy, y_peer(d)).start()
    s.ybuf[yy] = s.part[yy]

    @pl.when(kk > 0)
    def _():
        full.forward(0, near_half)

    @pl.when(kk == 0)
    def _():
        early.forward(0, 1)

    for d in range(1, ny):
        py_copy(y_peer(d), yy).wait_recv()
    acc_y, lse_y = merge(s.ybuf[...].reshape(ny, nz * 8, 128))
    s.zsend[...] = encode(acc_y, lse_y).reshape(s.zsend.shape)

    def pz_copy(src_z, dst_z):
        return remote(
            s.zsend.at[dst_z], s.zbuf.at[src_z], s.s_pz.at[dst_z], s.r_pz.at[src_z], at(yy, dst_z)
        )

    loop(1, nz, lambda i: pz_copy(zz, nth_z(nz - i)).start())
    s.zbuf[zz] = s.zsend[zz]
    weights_middle()

    @pl.when(kk == 0)
    def _():
        early.forward(1, nz)

    loop(1, nz, lambda d: pz_copy(z_peer(d), zz).wait_recv())
    attn, _ = merge(s.zbuf[...])
    attn = attn.astype(BF16).astype(F32)
    pair = jnp.where(sub8 < 4, attn, 0.0).astype(BF16)
    last = jnp.where((sub8 < 4) & (lane8 < 64), pltpu.roll(attn, 4, 0), 0.0).astype(BF16)
    dec = jnp.dot(pair, s.w[0:128, :], preferred_element_type=F32)
    dec = dec + jnp.dot(last[:, :64], s.w[128:192, :], preferred_element_type=F32)
    s.decsend[...] = folded_rows(dec, 0).astype(BF16)

    def dec_copy(src_k):
        return remote(s.decsend, s.decbuf.at[src_k], s.s_dec.at[0], s.r_dec.at[src_k], {"kv": 0})

    def finished(mixed):
        square = jnp.sum(mixed * mixed, axis=1, keepdims=True) / width
        s.fsend[...] = (mixed * lax.rsqrt(square + EPSILON) * s.gains[...][1:2]).astype(BF16)

    @pl.when(kk != 0)
    def _():
        dec_copy(kk).start()
        if nz > near_half:
            full.forward(near_half, nz)
        weights_last()
        full.experts()
        full.sums()
        finished(s.middle[...] + full.collect())

    @pl.when(kk == 0)
    def _():
        decoded = s.decsend[...].astype(F32)
        for k in range(1, nkv):
            dec_copy(k).wait_recv()
            decoded = decoded + s.decbuf[k].astype(F32)
        spread4 = jnp.concatenate([decoded, pltpu.roll(decoded, 4, 0)], axis=1)
        middle = s.middle[...] + jnp.where(iota((8, width), 0) < 4, spread4, 0.0)
        s.middle[...] = middle
        rows4 = folded_rows(normed_rows(middle), 0).astype(BF16)
        late.send(jnp.concatenate([rows4, s.route[...]], axis=1))
        weights_last()
        early.experts()
        late.forward(0, nz)
        early.sums()
        late.experts()
        late.sums()
        first, last = late.collect(), early.collect()
        low = jnp.where(low4, first, pltpu.roll(last, 4, 0))
        high = jnp.where(low4, pltpu.roll(first, 4, 0), last)
        finished(s.middle[...] + jnp.concatenate([low, high], axis=1))

    def f_copy(src_k, dst_k):
        start = pl.multiple_of(128 * (3 * (dst_k // 2) + lax.rem(dst_k, 2)), 128)
        return remote(
            s.fsend.at[:, pl.ds(start, 256)],
            s.fbuf.at[src_k],
            s.s_f.at[dst_k],
            s.r_f.at[src_k],
            {"kv": dst_k},
        )

    for d in range(1, nkv):
        f_copy(kk, k_peer(d)).start()
    s.fbuf[kk] = s.fsend[:, pl.ds(pl.multiple_of(128 * (3 * xx + cc), 128), 256)]

    def z_sent(d):
        peer = z_peer(d)
        q_copy(zz, peer).wait_send()
        pz_copy(zz, peer).wait_send()

    loop(1, nz, z_sent)
    for d in range(1, ny):
        peer = y_peer(d)
        qy_copy(yy, peer).wait_send()
        py_copy(yy, peer).wait_send()

    @pl.when(kk != 0)
    def _():
        dec_copy(kk).wait_send()
        full.finish()

    @pl.when(kk == 0)
    def _():
        early.finish()
        late.finish()

    for d in range(1, nkv):
        peer = k_peer(d)
        res_copy(kk, peer).wait_send()
        g_copy(kk, peer).wait_send()
        rs_copy(kk, peer).wait_send()
    for copy in own_copies():
        copy.wait_send()
    for copy in half_copies(3, 3) + half_copies(1, 4):
        copy.wait_send()
    for copy in share_copies(3, 5) + share_copies(1, 6) + share_copies(2, 7):
        copy.wait_send()

    for d in range(1, nkv):
        f_copy(k_peer(d), kk).wait_recv()
    s.out_v[...] = jnp.dot(
        s.fbuf[...].reshape(nkv * 8, 256), placement(cc, True), preferred_element_type=F32
    ).astype(BF16)
    for d in range(1, nkv):
        f_copy(kk, k_peer(d)).wait_send()


INPUTS = ("res", "q", "pre", "kv", "pt", "len", "w", "gi", "go", "ids", "rw", "st", "wgu", "wd")
PASS_SCRATCH = (
    "x",
    "o",
    "oy",
    "os",
    "ob",
    "s_xz",
    "r_xz",
    "s_xr",
    "s_xy",
    "r_xy",
    "s_oy",
    "r_oy",
    "s_oz",
    "r_oz",
)
LOADED = ("q", "res", "gi", "go", "pre", "w", "ids", "rw", "st", "pt", "len", "kv")


def dma(*shape):
    return pltpu.SemaphoreType.DMA(shape)


def local(
    npg,
    nkv,
    residual_in,
    queries,
    prefill_attn,
    kv_cache,
    page_table,
    lengths,
    out_weight,
    norm_gain_in,
    norm_gain_out,
    expert_ids,
    route_weight,
    slot_table,
    w_gate_up,
    w_down,
):
    ny, nz = NY, npg // NY
    width = out_weight.shape[1]
    ff2, ff = w_gate_up.shape[2], w_down.shape[1]
    groups = min(4, nz)
    args = (
        residual_in,
        queries,
        prefill_attn,
        kv_cache.reshape(kv_cache.shape[0], kv_cache.shape[2], kv_cache.shape[3]),
        page_table.T,
        lengths.reshape(1, -1),
        out_weight,
        norm_gain_in.reshape(1, -1),
        norm_gain_out.reshape(1, -1),
        expert_ids.T,
        route_weight.T,
        slot_table.T,
        w_gate_up,
        w_down.swapaxes(1, 2),
    )
    by_name = dict(zip(INPUTS, args))
    V = pltpu.VMEM
    scratch = {name: V(by_name[name].shape, by_name[name].dtype) for name in LOADED}
    scratch.update(
        wgu=V((nkv, 192, ff2), BF16),
        wd=V((nkv, 192, ff), BF16),
        qtile=V((16, 128), F32),
        gtile=V((16, 256), F32),
        qall=V((ny, nz, 8, 128), BF16),
        select=V((by_name["kv"].shape[0] * 8, npg * 8), BF16),
        part=V((ny, nz, 8, 128), BF16),
        scatter=V((npg * 8, by_name["kv"].shape[0] * 8), BF16),
        owner_row=V((1, by_name["kv"].shape[0] * 8), F32),
        ybuf=V((ny, nz, 8, 128), BF16),
        zsend=V((nz, 8, 128), BF16),
        zbuf=V((nz, 8, 128), BF16),
        pre_s=V((72, 192), F32),
        decsend=V((8, width // 2), BF16),
        decbuf=V((nkv, 8, width // 2), BF16),
        s_dec=dma(1),
        r_dec=dma(nkv),
        proj=V((nkv, 8, width), BF16),
        rsbuf=V((nkv, 8, width), BF16),
        ressend=V((nkv, 8, 256), BF16),
        resbuf=V((nkv, 8, 256), BF16),
        gsend=V((8, 256), F32),
        gbuf=V((nkv, 8, 256), F32),
        turn=V((8, 128), F32),
        ids_t=V((128, 8), F32),
        rw_t=V((128, 8), F32),
        route=V((8, 128), BF16),
        middle=V((8, width), F32),
        gains=V((8, width), F32),
        normed=V((8, width), F32),
        fsend=V((8, width), BF16),
        fbuf=V((nkv, 8, 256), BF16),
        l_in=dma(len(LOADED)),
        l_w=dma(2),
        s_wg=dma(8),
        s_wd=dma(8),
        r_wg=dma(nkv),
        r_wd=dma(nkv),
        r_fg=dma(2),
        r_fd=dma(2),
    )
    for name, n in (
        ("q", nz),
        ("pz", nz),
        ("qy", ny),
        ("py", ny),
        ("rs", nkv),
        ("res", nkv),
        ("g", nkv),
        ("f", nkv),
    ):
        scratch["s_" + name] = dma(n)
        scratch["r_" + name] = dma(n)
    for tag, cols in (("a", width), ("b", width // 2), ("c", width // 2)):
        shapes = dict(
            x=V((ny, nz, 8, cols + 128), BF16),
            o=V((ny, nz, 8, cols), BF16),
            oy=V((ny, nz, 8, cols), BF16),
            os=V((nz, 8, cols), BF16),
            ob=V((nz, 8, cols), BF16),
            s_xz=dma(nz),
            r_xz=dma(nz),
            s_xr=dma(8),
            s_xy=dma(ny, nz),
            r_xy=dma(ny, nz),
            s_oy=dma(ny, groups),
            r_oy=dma(ny, groups),
            s_oz=dma(nz),
            r_oz=dma(nz),
        )
        scratch.update({name + "_" + tag: shape for name, shape in shapes.items()})
    names = [name + "_in" for name in INPUTS] + ["out_v"] + list(scratch)
    return pl.pallas_call(
        functools.partial(layer_kernel, nz, nkv, names),
        out_shape=jax.ShapeDtypeStruct(residual_in.shape, BF16),
        in_specs=[pl.BlockSpec(memory_space=pltpu.HBM)] * len(args),
        out_specs=pl.BlockSpec(memory_space=pltpu.VMEM),
        scratch_shapes=list(scratch.values()),
        compiler_params=pltpu.CompilerParams(
            collective_id=0, has_side_effects=True, vmem_limit_bytes=56 << 20
        ),
        name="layer",
    )(*args)


def solution(mesh):
    in_specs = (
        P("pg", "kv"),
        P("pg", "kv"),
        P("pg", "kv"),
        P("pg", "kv", None, None),
        P(),
        P(),
        P("kv", None),
        P("kv"),
        P("kv"),
        P("pg", None),
        P("pg", None),
        P(),
        P("pg", "kv", None),
        P("pg", None, "kv"),
    )
    body = functools.partial(local, mesh.shape["pg"], mesh.shape["kv"])
    return jax.shard_map(
        body, mesh=mesh, in_specs=in_specs, out_specs=P("pg", "kv"), check_vma=False
    )
```
